256 devices in a mesh: stn: 8 (over x_hi, y), tm: 16 (over z, core), cores: 2 (over x_lo).
Axes of the slice: x: 4 (x_hi: 2, x_lo: 2; x = x_hi * 2 + x_lo), y: 4, z: 8, core: 2. Of those that a mesh axis runs over, the one named last changes fastest.
Arguments:
- samples: bfloat16 [64, 4194304], P('stn', ('tm', 'cores')), may hold values from -6 to 6
- delays: int32 [64], P('stn'), may hold values from 0 to 32768, as said below
- valid: int32 [64], P('stn'), may hold values 0 or 1
- tone_chan: int32 [64, 64], P('stn'), may hold values from 0 to 16383
Outputs:
- visibility: float32 [16384, 8192], P(('stn', 'tm', 'cores'))
- phase_cal: float32 [64, 128], P('stn')
The draws below stay inside these ranges and needn't reach their ends.
Inputs may be any that keep to these rules, and one draw needn't show every extreme that they name: `delays`: each station's delay in samples; some station has a delay of exactly 32768.
All inputs are finite; a program needn't handle non-finite values. No bound on the sum of `valid` on one device may be relied on, other than what follows from the above.
Results may differ from the reference program's by a relative error of at most 0.007.
Values may be sent and summed in bfloat16 or wider, within the bound.
No kernel may reach another device: no remote copies, remote signals or barrier semaphores. Data moves between devices by JAX's collectives and lax.ppermute only.
A program may use at most 128 MiB of HBM per device.

```python
import math
import jax
import jax.numpy as jnp
from jax import lax

S = 64
NCH = 16384
FA = 256
FB = 128
NTONE = 64
SPECTRA = 128
SAMPLES = 4194304
MAXD = 32768


def draw_delays(key, part):
    base = jax.random.fold_in(key, 17)
    key_one, key_two = jax.random.split(base)
    values = jax.random.randint(key_one, (S,), 0, MAXD + 1)
    chosen = jax.random.randint(key_two, (), 0, S)
    return jnp.where(jnp.arange(S) == chosen, MAXD, values).astype(jnp.int32)


def with_ends(values, rng, least, top_value):
    dims = values.shape
    index_at = [jax.random.randint(jax.random.fold_in(rng, axis), (), 0, dims[axis]) for axis in range(len(dims))]
    values = values.at[tuple(index_at)].set(least)
    longest = dims.index(max(dims))
    index_at[longest] = (index_at[longest] + 1) % dims[longest]
    return values.at[tuple(index_at)].set(top_value)


def shard_levels(key, dims, cuts, smallest, top_value):
    def one(dim, parts):
        heights = jax.random.uniform(jax.random.fold_in(jax.random.fold_in(key, 6), dim), (parts,), jnp.float32, smallest / len(cuts), top_value / len(cuts))
        return jnp.repeat(jnp.exp(heights), dims[dim] // parts).reshape((-1,) + (1,) * (len(dims) - dim - 1))

    level = one(*cuts[0])
    for cut in cuts[1:]:
        level = level * one(*cut)
    return level


def noise(stream_key, shape, width, limit, cuts=(), kind=jnp.bfloat16):
    array = jax.random.normal(stream_key, shape, jnp.float32) * width
    if len(cuts) > 0:
        array = shard_levels(stream_key, shape, cuts, -0.22, 0.18) * array
    return jnp.clip(array, min=-limit, max=limit).astype(kind)


def setup_inputs(seed: int = 0) -> dict:
    arg_keys = jax.random.split(jax.random.key(seed), 5)
    return {
        "samples": noise(arg_keys[0], (S, SAMPLES), 1.0, 6.0, ((0, 8), (1, 32))),
        "delays": draw_delays(jax.random.fold_in(arg_keys[4], 71), 0),
        "valid": with_ends((jax.random.randint(arg_keys[2], (S,), 0, 4) < 3).astype(jnp.int32), jax.random.fold_in(arg_keys[2], 1), 0, 1),
        "tone_chan": with_ends(jax.random.randint(arg_keys[3], (S, NTONE), 0, NCH), jax.random.fold_in(arg_keys[3], 1), 0, NCH - 1).astype(jnp.int32),
    }


def make_tables():
    outer_idx = jnp.arange(FA, dtype=jnp.int32)
    phases = outer_idx[:, None] * outer_idx[None, :] % FA
    angles = 2.0 * math.pi / FA * phases.astype(jnp.float32)
    section_one = jnp.stack([jnp.cos(angles), -jnp.sin(angles)]).astype(jnp.bfloat16)
    inner_idx = jnp.arange(FB, dtype=jnp.int32)
    spectrum_len = FA * FB
    twist_idx = outer_idx[:, None] * inner_idx[None, :] % spectrum_len
    twists = 2.0 * math.pi / spectrum_len * twist_idx.astype(jnp.float32)
    norm_scale = 1.0 / math.sqrt(spectrum_len)
    twist_cos = jnp.cos(twists) * norm_scale
    twist_sin = jnp.sin(twists) * norm_scale
    half_idx = jnp.arange(FB // 2, dtype=jnp.int32)
    last_idx = inner_idx[:, None] * half_idx[None, :] % FB
    thetas = 2.0 * math.pi / FB * last_idx.astype(jnp.float32)
    cosine = jnp.cos(thetas)
    sine_val = jnp.sin(thetas)
    section_two = jnp.stack([jnp.stack([cosine, -sine_val], axis=1), jnp.stack([sine_val, cosine], axis=1)]).astype(jnp.bfloat16)
    return (section_one, twist_cos, twist_sin, section_two)

def channelize(window, usable, tables):
    section_one, twist_cos, twist_sin, section_two = tables
    spec_count = window.shape[0] // (FA * FB)
    blocks = window.reshape(spec_count, FA, FB).astype(jnp.float32)
    section_out = jnp.einsum('xkn,bnm->bxkm', section_one.astype(jnp.float32), blocks)
    real_part = section_out[:, 0] * twist_cos + section_out[:, 1] * twist_sin
    imag_part = section_out[:, 1] * twist_cos - section_out[:, 0] * twist_sin
    twisted = jnp.stack([real_part, imag_part], axis=1).astype(jnp.bfloat16)
    twisted = lax.optimization_barrier(twisted).astype(jnp.float32)
    product = jnp.einsum('xnrq,bxkn->brqk', section_two.astype(jnp.float32), twisted)
    return (product.reshape(spec_count, 2, NCH) * usable).astype(jnp.bfloat16)

def reference(samples, delays, valid, tone_chan):
    tables = make_tables()
    stretch = samples.shape[1]

    def station(inputs):
        stream, shift_by, usable, tone_ids = inputs
        padded = jnp.concatenate([stream, jnp.zeros((MAXD,), stream.dtype)])
        window = lax.dynamic_slice_in_dim(padded, shift_by.astype(jnp.int32), stretch)
        spectra = channelize(window, usable.astype(jnp.float32), tables)
        widened = lax.optimization_barrier(spectra).astype(jnp.float32)
        totals = lax.optimization_barrier(jnp.sum(widened, axis=0))
        picked = jnp.take(totals, tone_ids, axis=1)
        return (spectra, picked.reshape(2 * NTONE))
    spectra, tone_picks = lax.map(station, (samples, delays, valid, tone_chan))
    norm_scale = 1.0 / math.sqrt(SPECTRA)
    phase_cal = tone_picks * norm_scale
    block_len = 128

    def gram_block(block_idx):
        piece_cut = lax.dynamic_slice_in_dim(spectra, block_idx * block_len, block_len, axis=3)
        widened = lax.optimization_barrier(piece_cut).astype(jnp.float32)
        rotated = jnp.stack([widened[:, :, 1], -widened[:, :, 0]], axis=2)
        stacked = jnp.stack([widened, rotated])
        gram_out = jnp.einsum('qitrc,jtrc->cqij', stacked, widened)
        return gram_out.reshape(block_len, 2 * S * S)
    visibility = lax.map(gram_block, jnp.arange(NCH // block_len, dtype=jnp.int32))
    visibility = visibility.reshape(NCH, 2 * S * S) * norm_scale
    return (visibility, phase_cal)
```

```python
import math

import jax
import jax.numpy as jnp
import ml_dtypes
import numpy as np
from jax import lax
from jax.experimental import pallas as pl
from jax.experimental.pallas import tpu as pltpu
from jax.sharding import PartitionSpec as P

S = 64
NCH = 16384
FA = 256
FB = 128
NTONE = 64
MAXD = 32768
NQ = FB // 2
NHI = 4
LO = FA // NHI
LANES = 128

f32 = jnp.float32
bf16 = jnp.bfloat16


def make_tables():
    k1 = np.arange(FA)
    angles = 2.0 * np.pi / FA * (k1[:, None] * k1[None, :] % FA)
    section_one = np.concatenate([np.cos(angles), -np.sin(angles)]).astype(ml_dtypes.bfloat16)
    n2 = np.arange(FB)
    length = FA * FB
    twists = 2.0 * np.pi / length * (k1[:, None] * n2[None, :] % length)
    scale = 1.0 / math.sqrt(length)
    twist_cos = (np.cos(twists) * scale).astype(np.float32)
    twist_sin = (np.sin(twists) * scale).astype(np.float32)
    q = np.arange(NQ)
    thetas = 2.0 * np.pi / FB * (q[:, None] * n2[None, :] % FB)
    section_two = np.concatenate([np.cos(thetas), np.sin(thetas)], axis=1).astype(
        ml_dtypes.bfloat16
    )
    return (section_one, twist_cos, twist_sin, section_two)


def f_kernel(
    delays, valid, x, halo, tones, one, tcos, tsin, two, msgs, picks, xs, obuf
):
    stations = x.shape[0]
    rows = x.shape[1] // LANES
    halo_rows = halo.shape[1] // LANES
    nt = rows // FA

    def spread(j, _):
        at = pl.multiple_of(j * LANES, LANES)
        xs[pl.ds(pl.multiple_of(j * stations, stations), stations), :] = x[
            :, pl.ds(at, LANES)
        ].astype(f32)
        return 0

    lax.fori_loop(0, rows, spread, 0, unroll=16)

    def spread_halo(j, _):
        at = pl.multiple_of(j * LANES, LANES)
        row = pl.multiple_of((rows + j) * stations, stations)
        xs[pl.ds(row, stations), :] = halo[:, pl.ds(at, LANES)].astype(f32)
        return 0

    lax.fori_loop(0, halo_rows, spread_halo, 0, unroll=16)
    xs[pl.ds((rows + halo_rows) * stations, stations), :] = jnp.zeros((stations, LANES), f32)

    def station(s, _):
        shift = delays[s]
        lead = shift // LANES
        within = shift - lead * LANES
        usable = valid[s].astype(f32)
        first = xs[pl.ds(lead * stations + s, rows, stride=stations), :]
        second = xs[pl.ds((lead + 1) * stations + s, rows, stride=stations), :]
        pair = jnp.concatenate([first.astype(bf16), second.astype(bf16)], axis=1)
        src = lax.broadcasted_iota(jnp.int32, (2 * LANES, LANES), 0)
        dst = lax.broadcasted_iota(jnp.int32, (2 * LANES, LANES), 1)
        move = (src == dst + within).astype(f32).astype(bf16)
        moved = jnp.dot(pair, move, preferred_element_type=f32).astype(bf16)
        tone = tones[pl.ds(s, 1), :]
        tone_q = tone // FA
        tone_k = tone - tone_q * FA
        col = lax.broadcasted_iota(jnp.int32, (2 * FA, 2 * NTONE), 0)
        lane = lax.broadcasted_iota(jnp.int32, (2 * FA, 2 * NTONE), 1)
        hi = col // (2 * LO)
        part = (col // LO) % 2
        chan = hi * LO + col % LO
        pick = ((chan == tone_k) & (part == lane // NTONE)).astype(f32).astype(bf16)
        total = jnp.zeros((NQ, 2 * NTONE), f32)
        for t in range(nt):
            block = moved[t * FA : (t + 1) * FA]
            section = jnp.dot(one[...], block, preferred_element_type=f32)
            re, im = section[:FA], section[FA:]
            cosine, sine = tcos[...], tsin[...]
            tr = re * cosine + im * sine
            ti = im * cosine - re * sine
            tr, ti, mr = tr.astype(bf16), ti.astype(bf16), (-tr).astype(bf16)
            real = jnp.concatenate([tr, ti], axis=1)
            imag = jnp.concatenate([ti, mr], axis=1)
            weights = jnp.concatenate(
                [p[h * LO : (h + 1) * LO] for h in range(NHI) for p in (real, imag)], axis=0
            )
            spec = lax.dot_general(
                two[...], weights, (((1,), (1,)), ((), ())), preferred_element_type=f32
            )
            spec = (spec * usable).astype(bf16)
            total = total + jnp.dot(spec, pick, preferred_element_type=f32)
            wide = spec.astype(f32)
            for h in range(NHI):
                at = pl.multiple_of(((h * nt + t) * stations + s) * NQ, NQ)
                obuf[pl.ds(at, NQ), :] = wide[:, h * LANES : (h + 1) * LANES]
        at_q = lax.broadcasted_iota(jnp.int32, (NQ, 2 * NTONE), 0)
        total = jnp.where(at_q == tone_q, total, 0.0)
        picks[pl.ds(s, 1), :] = jnp.sum(total, axis=0, keepdims=True)
        return 0

    lax.fori_loop(0, stations, station, 0)

    def gather(q, _):
        for h in range(NHI):
            got = obuf[pl.ds(h * nt * stations * NQ + q, nt * stations, stride=NQ), :]
            msgs[q * NHI + h] = got.astype(bf16)
        return 0

    lax.fori_loop(0, NQ, gather, 0, unroll=4)


def channelized(samples, trailing, delays, valid, tones, tables):
    stations, stretch = samples.shape
    rows = stretch // LANES
    nt = rows // FA
    smem = pl.BlockSpec(memory_space=pltpu.SMEM)
    vmem = pl.BlockSpec(memory_space=pltpu.VMEM)
    return pl.pallas_call(
        f_kernel,
        out_shape=(
            jax.ShapeDtypeStruct((NQ * NHI, nt * stations, LANES), bf16),
            jax.ShapeDtypeStruct((stations, 2 * NTONE), f32),
        ),
        in_specs=[smem, smem] + [vmem] * 7,
        out_specs=(vmem, vmem),
        scratch_shapes=[
            pltpu.VMEM(((rows + trailing.shape[1] // LANES + 1) * stations, LANES), f32),
            pltpu.VMEM((NHI * nt * stations * NQ, LANES), f32),
        ],
        compiler_params=pltpu.CompilerParams(vmem_limit_bytes=56 << 20),
        name="channelize",
    )(delays, valid, samples, trailing, tones, *tables)


PITCH = 136


def x_kernel(norm_scale, per_source, recv, vis, rs, ts, gs):
    sources, rows, _ = recv.shape
    local = per_source
    groups = S // local
    times = sources // groups * rows // local

    def widen(i, _):
        at = pl.multiple_of(i * rows, rows)
        rs[pl.ds(at, rows), :] = recv[i].astype(f32)
        return 0

    lax.fori_loop(0, sources, widen, 0, unroll=8)

    def turn(i, _):
        g = i // local
        s = i - g * local
        got = rs[pl.ds(g * times * local + s, times, stride=local), :]
        ts[pl.ds(pl.multiple_of(i * PITCH, 8), LANES), :] = got.T
        return 0

    lax.fori_loop(0, S, turn, 0, unroll=4)

    lane = lax.broadcasted_iota(jnp.int32, (8, LANES), 1)

    def eight(o, _):
        base = o * 8
        for c in range(8):
            re = ts[pl.ds(base + c, S, stride=PITCH), :]
            im = ts[pl.ds(base + c + LO, S, stride=PITCH), :]
            plus, quad, minus = re.astype(bf16), im.astype(bf16), (-re).astype(bf16)
            straight = jnp.concatenate([plus, quad], axis=1)
            turned = jnp.concatenate([quad, minus], axis=1)
            left = jnp.concatenate([straight, turned], axis=0)
            right = jnp.concatenate([straight, straight], axis=0)
            gram = lax.dot_general(
                left, right, (((1,), (1,)), ((), ())), preferred_element_type=f32
            )
            gs[pl.ds(c * PITCH, 2 * S), :] = gram * norm_scale
        top = pl.multiple_of(base, 8)
        for j in range(S):
            even = gs[pl.ds(2 * j, 8, stride=PITCH), :]
            odd = gs[pl.ds(2 * j + 1, 8, stride=PITCH), :]
            vis[pl.ds(top, 8), pl.ds(j * LANES, LANES)] = jnp.where(lane < S, even, odd)
        return 0

    lax.fori_loop(0, LO // 8, eight, 0)


def correlated(recv, per_source, norm_scale):
    vmem = pl.BlockSpec(memory_space=pltpu.VMEM)
    sources, rows, _ = recv.shape
    return pl.pallas_call(
        lambda *refs: x_kernel(norm_scale, per_source, *refs),
        out_shape=jax.ShapeDtypeStruct((LO, 2 * S * S), f32),
        in_specs=[vmem],
        out_specs=vmem,
        scratch_shapes=[
            pltpu.VMEM((sources * rows, LANES), f32),
            pltpu.VMEM((S * PITCH, LANES), f32),
            pltpu.VMEM((8 * PITCH, LANES), f32),
        ],
        compiler_params=pltpu.CompilerParams(vmem_limit_bytes=56 << 20),
        name="correlate",
    )(recv)


def passed_along(block, axis, distance):
    devices = range(lax.axis_size(axis))
    route = [(i - distance, i) for i in devices if i - distance in devices]
    return lax.ppermute(block, axis, route)


def summed(value):
    for axis in ("cores", "tm"):
        size = lax.axis_size(axis)
        step = 1
        while step < size:
            value = value + lax.ppermute(value, axis, [(i, i ^ step) for i in range(size)])
            step *= 2
    return value


def shards(samples, delays, valid, tone_chan):
    tables = make_tables()
    stations, stretch = samples.shape
    trailing = passed_along(samples[:, :MAXD], ("tm", "cores"), -1)
    tones = jnp.concatenate([tone_chan, tone_chan], axis=1)
    msgs, picks = channelized(samples, trailing, delays, valid, tones, tables)
    spectra_all = stretch // (FA * FB) * lax.axis_size("tm") * lax.axis_size("cores")
    norm_scale = 1.0 / math.sqrt(spectra_all)
    phase_cal = summed(picks) * norm_scale
    recv = lax.all_to_all(msgs, ("stn", "tm", "cores"), split_axis=0, concat_axis=0, tiled=True)
    return (correlated(recv, stations, norm_scale), phase_cal)


def solution(mesh):
    return jax.shard_map(
        shards,
        mesh=mesh,
        in_specs=(P("stn", ("tm", "cores")), P("stn"), P("stn"), P("stn", None)),
        out_specs=(P(("stn", "tm", "cores"), None), P("stn", None)),
        check_vma=False,
    )
```

```python
import math

import jax
import jax.numpy as jnp
import ml_dtypes
import numpy as np
from jax import lax
from jax.experimental import pallas as pl
from jax.experimental.pallas import tpu as pltpu
from jax.sharding import PartitionSpec as P

S = 64
NCH = 16384
FA = 256
FB = 128
NTONE = 64
MAXD = 32768
NQ = FB // 2
NHI = 4
LO = FA // NHI
LANES = 128

f32 = jnp.float32
bf16 = jnp.bfloat16


def make_tables():
    k1 = np.arange(FA)
    angles = 2.0 * np.pi / FA * (k1[:, None] * k1[None, :] % FA)
    section_one = np.concatenate([np.cos(angles), -np.sin(angles)], axis=1).astype(
        ml_dtypes.bfloat16
    )
    n2 = np.arange(FB)
    length = FA * FB
    twists = 2.0 * np.pi / length * (n2[:, None] * k1[None, :] % length)
    scale = 1.0 / math.sqrt(length)
    twist_cos = (np.cos(twists) * scale).astype(np.float32)
    twist_sin = (np.sin(twists) * scale).astype(np.float32)
    q = np.arange(NQ)
    thetas = 2.0 * np.pi / FB * (q[:, None] * n2[None, :] % FB)
    cosine, sine = np.cos(thetas), np.sin(thetas)
    section_two = np.block([[cosine, sine], [-sine, cosine]]).astype(ml_dtypes.bfloat16)
    return (section_one, twist_cos, twist_sin, section_two)


OPITCH = NQ + 8
PIECES = 4


def f_kernel(nt, n_in, at_row, delays, valid, *refs):
    streams = refs[:n_in]
    before, tones, one, tcos, tsin, two = refs[n_in : n_in + 6]
    msgs, picks, xin, xs, obuf, mbuf, in_sem, out_sem = refs[-8:]
    stations = tones.shape[0]
    rows = nt * FA
    chunk = FA * LANES
    chunks = xin.shape[1] // chunk
    pitch = xs.shape[0] // stations
    copies = []
    for stream in streams:
        for k in range(stream.shape[1] // chunk):
            i = len(copies)
            copies.append(
                pltpu.make_async_copy(
                    stream.at[:, pl.ds(k * chunk, chunk)],
                    xin.at[:, pl.ds(i * chunk, chunk)],
                    in_sem.at[i],
                )
            )
            copies[-1].start()
    for i in range(chunks):
        copies[i].wait()

        def spread(j, _):
            at = pl.multiple_of(j * LANES, LANES)
            xs[pl.ds(j, stations, stride=pitch), :] = xin[:, pl.ds(at, LANES)].astype(f32)
            return 0

        lax.fori_loop(i * FA, (i + 1) * FA, spread, 0, unroll=16)
    xs[pl.ds(chunks * FA, stations, stride=pitch), :] = jnp.zeros((stations, LANES), f32)
    src = lax.broadcasted_iota(jnp.int32, (2 * LANES, LANES), 0)
    dst = lax.broadcasted_iota(jnp.int32, (2 * LANES, LANES), 1)
    low = lax.broadcasted_iota(jnp.int32, (NQ, LANES), 1) < LO
    at_q = lax.broadcasted_iota(jnp.int32, (NQ, 2 * NTONE), 0)
    in_re = lax.broadcasted_iota(jnp.int32, (NQ, 2 * NTONE), 1) < NTONE
    col = lax.broadcasted_iota(jnp.int32, (FA, 2 * NTONE), 0)

    def station(s, _):
        shift = delays[s]
        lead = shift // LANES
        within = shift - lead * LANES
        usable = valid[s].astype(f32)
        first = xs[pl.ds(s * pitch + lead, rows), :]
        second = xs[pl.ds(s * pitch + lead + 1, rows), :]
        pair = jnp.concatenate([first.astype(bf16), second.astype(bf16)], axis=1)
        move = (src == dst + within).astype(f32).astype(bf16)
        moved = jnp.dot(pair, move, preferred_element_type=f32).astype(bf16)
        last = (two[...].astype(f32) * usable).astype(bf16)
        kept = []
        for t in range(nt):
            block = moved[t * FA : (t + 1) * FA]
            section = lax.dot_general(
                block, one[...], (((0,), (0,)), ((), ())), preferred_element_type=f32
            )
            re, im = section[:, :FA], section[:, FA:]
            cosine, sine = tcos[...], tsin[...]
            tr = (re * cosine + im * sine).astype(bf16)
            ti = (im * cosine - re * sine).astype(bf16)
            spec = jnp.dot(
                last, jnp.concatenate([tr, ti], axis=0), preferred_element_type=f32
            )
            kept.append(spec.astype(bf16))
            for j in range(FA // LANES):
                a = spec[:NQ, j * LANES : (j + 1) * LANES]
                b = spec[NQ:, j * LANES : (j + 1) * LANES]
                even = jnp.where(low, a, pltpu.roll(b, LO, 1))
                odd = jnp.where(low, pltpu.roll(a, LO, 1), b)
                for h, piece in ((2 * j, even), (2 * j + 1, odd)):
                    at = pl.multiple_of(((h * nt + t) * stations + s) * OPITCH, 8)
                    obuf[pl.ds(at, NQ), :] = piece
        tone = tones[pl.ds(s, 1), :]
        tone_q = tone // FA
        tone_k = tone - tone_q * FA
        pick = (col == tone_k).astype(f32).astype(bf16)
        found = jnp.dot(jnp.concatenate(kept, axis=0), pick, preferred_element_type=f32)
        total = jnp.zeros((NQ, 2 * NTONE), f32)
        for t in range(nt):
            own = found[2 * t * NQ : 2 * (t + 1) * NQ]
            total = total + jnp.where(in_re, own[:NQ], own[NQ:])
        total = jnp.where(at_q == tone_q, total, 0.0)
        picks[pl.ds(s, 1), :] = before[pl.ds(s, 1), :] + jnp.sum(total, axis=0, keepdims=True)
        return 0

    lax.fori_loop(0, stations, station, 0)

    per = NQ // PIECES
    sent = []
    for i in range(PIECES):

        def gather(q, _):
            for h in range(NHI):
                got = obuf[
                    pl.ds(h * nt * stations * OPITCH + q, nt * stations, stride=OPITCH), :
                ]
                mbuf[q * NHI + h] = got.astype(bf16)
            return 0

        lax.fori_loop(i * per, (i + 1) * per, gather, 0, unroll=4)
        span = pl.ds(i * per * NHI, per * NHI)
        sent.append(
            pltpu.make_async_copy(
                mbuf.at[span], msgs.at[span, pl.ds(at_row, nt * stations), :], out_sem.at[i]
            )
        )
        sent[-1].start()
    for copy in sent:
        copy.wait()


def channelized(streams, nt, at_row, total_rows, delays, valid, before, tones, tables, msgs=None):
    stations = tones.shape[0]
    smem = pl.BlockSpec(memory_space=pltpu.SMEM)
    vmem = pl.BlockSpec(memory_space=pltpu.VMEM)
    hbm = pl.BlockSpec(memory_space=pl.ANY)
    length = sum(stream.shape[1] for stream in streams)
    pitch = (length // LANES // 16 + 1) * 16 + 8
    args = (delays, valid, *streams, before, tones, *tables)
    specs = [smem, smem] + [hbm] * len(streams) + [vmem] * 6
    aliases = {}
    if msgs is not None:
        aliases = {len(args): 0}
        args += (msgs,)
        specs += [hbm]
    return pl.pallas_call(
        lambda *refs: f_kernel(nt, len(streams), at_row, *refs),
        out_shape=(
            jax.ShapeDtypeStruct((NQ * NHI, total_rows, LANES), bf16),
            jax.ShapeDtypeStruct((stations, 2 * NTONE), f32),
        ),
        in_specs=specs,
        out_specs=(hbm, vmem),
        scratch_shapes=[
            pltpu.VMEM((stations, length), bf16),
            pltpu.VMEM((stations * pitch, LANES), f32),
            pltpu.VMEM((NHI * nt * stations * OPITCH, LANES), f32),
            pltpu.VMEM((NQ * NHI, nt * stations, LANES), bf16),
            pltpu.SemaphoreType.DMA((length // (FA * LANES),)),
            pltpu.SemaphoreType.DMA((PIECES,)),
        ],
        input_output_aliases=aliases,
        compiler_params=pltpu.CompilerParams(vmem_limit_bytes=56 << 20),
        name="channelize",
    )(*args)


PITCH = 136


def x_kernel(norm_scale, per_source, recv, vis, rs, ts, gs):
    sources, rows, _ = recv.shape
    local = per_source
    groups = S // local
    times = sources // groups * rows // local

    def widen(i, _):
        at = pl.multiple_of(i * rows, rows)
        rs[pl.ds(at, rows), :] = recv[i].astype(f32)
        return 0

    lax.fori_loop(0, sources, widen, 0, unroll=8)

    def turn(i, _):
        g = i // local
        s = i - g * local
        got = rs[pl.ds(g * times * local + s, times, stride=local), :]
        ts[pl.ds(pl.multiple_of(i * PITCH, 8), LANES), :] = got.T
        return 0

    lax.fori_loop(0, S, turn, 0, unroll=4)

    lane = lax.broadcasted_iota(jnp.int32, (8, LANES), 1)

    def eight(o, _):
        base = o * 8
        for c in range(8):
            re = ts[pl.ds(base + c, S, stride=PITCH), :]
            im = ts[pl.ds(base + c + LO, S, stride=PITCH), :]
            plus, quad, minus = re.astype(bf16), im.astype(bf16), (-re).astype(bf16)
            straight = jnp.concatenate([plus, quad], axis=1)
            turned = jnp.concatenate([quad, minus], axis=1)
            left = jnp.concatenate([straight, turned], axis=0)
            right = jnp.concatenate([straight, straight], axis=0)
            gram = lax.dot_general(
                left, right, (((1,), (1,)), ((), ())), preferred_element_type=f32
            )
            gs[pl.ds(c * PITCH, 2 * S), :] = gram * norm_scale
        top = pl.multiple_of(base, 8)
        for j in range(S):
            even = gs[pl.ds(2 * j, 8, stride=PITCH), :]
            odd = gs[pl.ds(2 * j + 1, 8, stride=PITCH), :]
            vis[pl.ds(top, 8), pl.ds(j * LANES, LANES)] = jnp.where(lane < S, even, odd)
        return 0

    lax.fori_loop(0, LO // 8, eight, 0)


def correlated(recv, per_source, norm_scale):
    vmem = pl.BlockSpec(memory_space=pltpu.VMEM)
    sources, rows, _ = recv.shape
    return pl.pallas_call(
        lambda *refs: x_kernel(norm_scale, per_source, *refs),
        out_shape=jax.ShapeDtypeStruct((LO, 2 * S * S), f32),
        in_specs=[vmem],
        out_specs=vmem,
        scratch_shapes=[
            pltpu.VMEM((sources * rows, LANES), f32),
            pltpu.VMEM((S * PITCH, LANES), f32),
            pltpu.VMEM((8 * PITCH, LANES), f32),
        ],
        compiler_params=pltpu.CompilerParams(vmem_limit_bytes=56 << 20),
        name="correlate",
    )(recv)


def passed_along(block, axis, distance):
    devices = range(lax.axis_size(axis))
    route = [(i - distance, i) for i in devices if i - distance in devices]
    return lax.ppermute(block, axis, route)


def summed(value, axis):
    size = lax.axis_size(axis)
    parts = [value]
    for step in range(1, size):
        parts.append(lax.ppermute(value, axis, [(i, (i + step) % size) for i in range(size)]))
    return sum(parts)


def shards(samples, delays, valid, tone_chan):
    tables = make_tables()
    stations, stretch = samples.shape
    whole = ("stn", "tm", "cores")
    here = stretch // (FA * FB)
    trailing = passed_along(samples[:, :MAXD], ("tm", "cores"), -1)
    tones = jnp.concatenate([tone_chan, tone_chan], axis=1)
    nothing = jnp.zeros((stations, 2 * NTONE), f32)
    most = here - 1
    rows = here * stations
    msgs, picks = channelized(
        [samples], most, 0, rows, delays, valid, nothing, tones, tables
    )
    msgs, picks = channelized(
        [samples[:, most * FA * FB :], trailing],
        1,
        most * stations,
        rows,
        delays,
        valid,
        picks,
        tones,
        tables,
        msgs,
    )
    spectra_all = here * lax.axis_size("tm") * lax.axis_size("cores")
    norm_scale = 1.0 / math.sqrt(spectra_all)
    recv = lax.all_to_all(msgs, whole, split_axis=0, concat_axis=0, tiled=True)
    phase_cal = summed(picks, ("tm", "cores")) * norm_scale
    return (correlated(recv, stations, norm_scale), phase_cal)


def solution(mesh):
    return jax.shard_map(
        shards,
        mesh=mesh,
        in_specs=(P("stn", ("tm", "cores")), P("stn"), P("stn"), P("stn", None)),
        out_specs=(P(("stn", "tm", "cores"), None), P("stn", None)),
        check_vma=False,
    )
```

```python
import math

import jax
import jax.numpy as jnp
import ml_dtypes
import numpy as np
from jax import lax
from jax.experimental import pallas as pl
from jax.experimental.pallas import tpu as pltpu
from jax.sharding import PartitionSpec as P

S = 64
NCH = 16384
FA = 256
FB = 128
NTONE = 64
MAXD = 32768
NQ = FB // 2
NHI = 4
LO = FA // NHI
LANES = 128

f32 = jnp.float32
bf16 = jnp.bfloat16


def make_tables():
    k1 = np.arange(FA)
    angles = 2.0 * np.pi / FA * (k1[:, None] * k1[None, :] % FA)
    section_one = np.concatenate([np.cos(angles), -np.sin(angles)], axis=1).astype(
        ml_dtypes.bfloat16
    )
    n2 = np.arange(FB)
    length = FA * FB
    twists = 2.0 * np.pi / length * (n2[:, None] * k1[None, :] % length)
    scale = 1.0 / math.sqrt(length)
    twist_cos = (np.cos(twists) * scale).astype(np.float32)
    twist_sin = (np.sin(twists) * scale).astype(np.float32)
    q = np.arange(NQ)
    thetas = 2.0 * np.pi / FB * (q[:, None] * n2[None, :] % FB)
    cosine, sine = np.cos(thetas), np.sin(thetas)
    section_two = np.block([[cosine, sine], [-sine, cosine]]).astype(ml_dtypes.bfloat16)
    return (section_one, twist_cos, twist_sin, section_two)


OPITCH = NQ + 8
PIECES = 4


def f_kernel(nt, span, at_row, more, delays, valid, *refs):
    stream, tones, one, tcos, tsin, two = refs[:6]
    trail, before = refs[6:8] if more else (None, None)
    msgs, picks, xin, xs, obuf, mbuf, in_sem, out_sem = refs[-8:]
    stations = tones.shape[0]
    rows = nt * FA
    chunk = FA * LANES
    pitch = xs.shape[0] // stations
    copies = []
    start, length = span
    for i in range(length // chunk):
        piece = pl.ds(i * chunk, chunk)
        copies.append(
            pltpu.make_async_copy(
                stream.at[:, pl.ds(start + i * chunk, chunk)], xin.at[:, piece], in_sem.at[i]
            )
        )
        copies[i].start()

    def spread_from(source, base):
        def spread(j, _):
            at = pl.multiple_of(j * LANES, LANES)
            xs[pl.ds(base + j, stations, stride=pitch), :] = source[:, pl.ds(at, LANES)].astype(
                f32
            )
            return 0

        return spread

    filled = length // LANES
    if more:
        lax.fori_loop(0, trail.shape[1] // LANES, spread_from(trail, filled), 0, unroll=16)
    for i in range(length // chunk):
        copies[i].wait()
        lax.fori_loop(i * FA, (i + 1) * FA, spread_from(xin, 0), 0, unroll=16)
    if more:
        filled += trail.shape[1] // LANES
    xs[pl.ds(filled, stations, stride=pitch), :] = jnp.zeros((stations, LANES), f32)
    src = lax.broadcasted_iota(jnp.int32, (2 * LANES, LANES), 0)
    dst = lax.broadcasted_iota(jnp.int32, (2 * LANES, LANES), 1)
    low = lax.broadcasted_iota(jnp.int32, (NQ, LANES), 1) < LO
    at_q = lax.broadcasted_iota(jnp.int32, (NQ, 2 * NTONE), 0)
    in_re = lax.broadcasted_iota(jnp.int32, (NQ, 2 * NTONE), 1) < NTONE
    col = lax.broadcasted_iota(jnp.int32, (FA, 2 * NTONE), 0)

    def station(s, _):
        shift = delays[s]
        lead = shift // LANES
        within = shift - lead * LANES
        usable = valid[s].astype(f32)
        first = xs[pl.ds(s * pitch + lead, rows), :]
        second = xs[pl.ds(s * pitch + lead + 1, rows), :]
        pair = jnp.concatenate([first.astype(bf16), second.astype(bf16)], axis=1)
        move = (src == dst + within).astype(f32).astype(bf16)
        moved = jnp.dot(pair, move, preferred_element_type=f32).astype(bf16)
        last = (two[...].astype(f32) * usable).astype(bf16)
        kept = []
        for t in range(nt):
            block = moved[t * FA : (t + 1) * FA]
            section = lax.dot_general(
                block, one[...], (((0,), (0,)), ((), ())), preferred_element_type=f32
            )
            re, im = section[:, :FA], section[:, FA:]
            cosine, sine = tcos[...], tsin[...]
            tr = (re * cosine + im * sine).astype(bf16)
            ti = (im * cosine - re * sine).astype(bf16)
            spec = jnp.dot(
                last, jnp.concatenate([tr, ti], axis=0), preferred_element_type=f32
            )
            kept.append(spec.astype(bf16))
            for j in range(FA // LANES):
                a = spec[:NQ, j * LANES : (j + 1) * LANES]
                b = spec[NQ:, j * LANES : (j + 1) * LANES]
                even = jnp.where(low, a, pltpu.roll(b, LO, 1))
                odd = jnp.where(low, pltpu.roll(a, LO, 1), b)
                for h, piece in ((2 * j, even), (2 * j + 1, odd)):
                    at = pl.multiple_of(((h * nt + t) * stations + s) * OPITCH, 8)
                    obuf[pl.ds(at, NQ), :] = piece
        tone = tones[pl.ds(s, 1), :]
        tone = jnp.concatenate([tone, tone], axis=1)
        tone_q = tone // FA
        tone_k = tone - tone_q * FA
        pick = (col == tone_k).astype(f32).astype(bf16)
        found = jnp.dot(jnp.concatenate(kept, axis=0), pick, preferred_element_type=f32)
        total = jnp.zeros((NQ, 2 * NTONE), f32)
        for t in range(nt):
            own = found[2 * t * NQ : 2 * (t + 1) * NQ]
            total = total + jnp.where(in_re, own[:NQ], own[NQ:])
        total = jnp.where(at_q == tone_q, total, 0.0)
        total = jnp.sum(total, axis=0, keepdims=True)
        if more:
            total = total + before[pl.ds(s, 1), :]
        picks[pl.ds(s, 1), :] = total
        return 0

    lax.fori_loop(0, stations, station, 0, unroll=2 if nt > 1 else stations)

    per = NQ // PIECES
    sent = []
    for i in range(PIECES):

        def gather(q, _):
            for h in range(NHI):
                got = obuf[
                    pl.ds(h * nt * stations * OPITCH + q, nt * stations, stride=OPITCH), :
                ]
                mbuf[q * NHI + h] = got.astype(bf16)
            return 0

        lax.fori_loop(i * per, (i + 1) * per, gather, 0, unroll=4)
        span = pl.ds(i * per * NHI, per * NHI)
        sent.append(
            pltpu.make_async_copy(
                mbuf.at[span], msgs.at[span, pl.ds(at_row, nt * stations), :], out_sem.at[i]
            )
        )
        sent[-1].start()
    for copy in sent:
        copy.wait()


def channelized(stream, span, nt, at_row, total_rows, delays, valid, tones, tables, trail=()):
    stations = tones.shape[0]
    smem = pl.BlockSpec(memory_space=pltpu.SMEM)
    vmem = pl.BlockSpec(memory_space=pltpu.VMEM)
    hbm = pl.BlockSpec(memory_space=pl.ANY)
    args = (delays, valid, stream, tones, *tables)
    specs = [smem, smem, hbm] + [vmem] * 5
    rows = span[1] // LANES
    aliases = {}
    if trail:
        after, msgs, picks = trail
        rows += after.shape[1] // LANES
        aliases = {len(args) + 2: 0}
        args += (pltpu.with_memory_space_constraint(after, pltpu.VMEM), picks, msgs)
        specs += [vmem, vmem, hbm]
    pitch = (rows // 16 + 1) * 16 + 8
    return pl.pallas_call(
        lambda *refs: f_kernel(nt, span, at_row, bool(trail), *refs),
        out_shape=(
            jax.ShapeDtypeStruct((NQ * NHI, total_rows, LANES), bf16),
            jax.ShapeDtypeStruct((stations, 2 * NTONE), f32),
        ),
        in_specs=specs,
        out_specs=(hbm, vmem),
        scratch_shapes=[
            pltpu.VMEM((stations, span[1]), bf16),
            pltpu.VMEM((stations * pitch, LANES), f32),
            pltpu.VMEM((NHI * nt * stations * OPITCH, LANES), f32),
            pltpu.VMEM((NQ * NHI, nt * stations, LANES), bf16),
            pltpu.SemaphoreType.DMA((span[1] // (FA * LANES),)),
            pltpu.SemaphoreType.DMA((PIECES,)),
        ],
        input_output_aliases=aliases,
        compiler_params=pltpu.CompilerParams(vmem_limit_bytes=56 << 20),
        name="channelize",
    )(*args)


PITCH = 136


def x_kernel(norm_scale, per_source, recv, vis, rs, ts, gs):
    sources, rows, _ = recv.shape
    local = per_source
    groups = S // local
    times = sources // groups * rows // local

    def widen(i, _):
        at = pl.multiple_of(i * rows, rows)
        rs[pl.ds(at, rows), :] = recv[i].astype(f32)
        return 0

    lax.fori_loop(0, sources, widen, 0, unroll=8)

    def turn(i, _):
        g = i // local
        s = i - g * local
        got = rs[pl.ds(g * times * local + s, times, stride=local), :]
        ts[pl.ds(pl.multiple_of(i * PITCH, 8), LANES), :] = got.T
        return 0

    lax.fori_loop(0, S, turn, 0, unroll=4)

    lane = lax.broadcasted_iota(jnp.int32, (8, LANES), 1)

    def eight(o, _):
        base = o * 8
        for c in range(8):
            re = ts[pl.ds(base + c, S, stride=PITCH), :]
            im = ts[pl.ds(base + c + LO, S, stride=PITCH), :]
            plus, quad, minus = re.astype(bf16), im.astype(bf16), (-re).astype(bf16)
            straight = jnp.concatenate([plus, quad], axis=1)
            turned = jnp.concatenate([quad, minus], axis=1)
            left = jnp.concatenate([straight, turned], axis=0)
            right = jnp.concatenate([straight, straight], axis=0)
            gram = lax.dot_general(
                left, right, (((1,), (1,)), ((), ())), preferred_element_type=f32
            )
            gs[pl.ds(c * PITCH, 2 * S), :] = gram * norm_scale
        top = pl.multiple_of(base, 8)
        for j in range(S):
            even = gs[pl.ds(2 * j, 8, stride=PITCH), :]
            odd = gs[pl.ds(2 * j + 1, 8, stride=PITCH), :]
            vis[pl.ds(top, 8), pl.ds(j * LANES, LANES)] = jnp.where(lane < S, even, odd)
        return 0

    lax.fori_loop(0, LO // 8, eight, 0)


def correlated(recv, per_source, norm_scale):
    vmem = pl.BlockSpec(memory_space=pltpu.VMEM)
    sources, rows, _ = recv.shape
    return pl.pallas_call(
        lambda *refs: x_kernel(norm_scale, per_source, *refs),
        out_shape=jax.ShapeDtypeStruct((LO, 2 * S * S), f32),
        in_specs=[vmem],
        out_specs=vmem,
        scratch_shapes=[
            pltpu.VMEM((sources * rows, LANES), f32),
            pltpu.VMEM((S * PITCH, LANES), f32),
            pltpu.VMEM((8 * PITCH, LANES), f32),
        ],
        compiler_params=pltpu.CompilerParams(vmem_limit_bytes=56 << 20),
        name="correlate",
    )(pltpu.with_memory_space_constraint(recv, pltpu.VMEM))


def passed_along(block, axis, distance):
    devices = range(lax.axis_size(axis))
    route = [(i - distance, i) for i in devices if i - distance in devices]
    return lax.ppermute(block, axis, route)


def joined(value, axis, steps):
    size = lax.axis_size(axis)
    parts = [value]
    for step in steps:
        parts.append(lax.ppermute(value, axis, [(i, i ^ step) for i in range(size)]))
    return sum(parts)


def shards(samples, delays, valid, tone_chan):
    tables = make_tables()
    stations, stretch = samples.shape
    whole = ("stn", "tm", "cores")
    section = FA * FB
    here = stretch // section
    most = here - 1
    rows = here * stations
    trailing = passed_along(samples[:, :MAXD], ("tm", "cores"), -1)
    own = (delays, valid, tone_chan, tables)
    early = channelized(samples, (0, stretch), most, 0, rows, *own)
    msgs, picks = channelized(
        samples,
        (most * section, section),
        1,
        most * stations,
        rows,
        *own,
        (trailing, *early),
    )
    spectra_all = here * lax.axis_size("tm") * lax.axis_size("cores")
    norm_scale = 1.0 / math.sqrt(spectra_all)
    recv = lax.all_to_all(msgs, whole, split_axis=0, concat_axis=0, tiled=True)
    picks = joined(picks, "cores", [1])
    picks = joined(picks, "tm", [1])
    picks = joined(picks, "tm", [2, 4, 6])
    recv, picks = lax.optimization_barrier((recv, picks))
    phase_cal = joined(picks, "tm", [8]) * norm_scale
    return (correlated(recv, stations, norm_scale), phase_cal)


def solution(mesh):
    return jax.shard_map(
        shards,
        mesh=mesh,
        in_specs=(P("stn", ("tm", "cores")), P("stn"), P("stn"), P("stn", None)),
        out_specs=(P(("stn", "tm", "cores"), None), P("stn", None)),
        check_vma=False,
    )
```

```python
import math

import jax
import jax.numpy as jnp
import ml_dtypes
import numpy as np
from jax import lax
from jax.experimental import pallas as pl
from jax.experimental.pallas import tpu as pltpu
from jax.sharding import PartitionSpec as P

S = 64
NCH = 16384
FA = 256
FB = 128
NTONE = 64
MAXD = 32768
NQ = FB // 2
NHI = 4
LO = FA // NHI
LANES = 128

f32 = jnp.float32
bf16 = jnp.bfloat16


def make_tables():
    k1 = np.arange(FA)
    angles = 2.0 * np.pi / FA * (k1[:, None] * k1[None, :] % FA)
    section_one = np.concatenate([np.cos(angles), -np.sin(angles)], axis=1).astype(
        ml_dtypes.bfloat16
    )
    n2 = np.arange(FB)
    length = FA * FB
    twists = 2.0 * np.pi / length * (n2[:, None] * k1[None, :] % length)
    scale = 1.0 / math.sqrt(length)
    twist_cos = (np.cos(twists) * scale).astype(np.float32)
    twist_sin = (np.sin(twists) * scale).astype(np.float32)
    q = np.arange(NQ)
    thetas = 2.0 * np.pi / FB * (q[:, None] * n2[None, :] % FB)
    cosine, sine = np.cos(thetas), np.sin(thetas)
    section_two = np.block([[cosine, sine], [-sine, cosine]]).astype(ml_dtypes.bfloat16)
    return (section_one, twist_cos, twist_sin, section_two)


OPITCH = NQ + 8
PIECES = 4
GROUP = (8, 2)
UNROLL = (1, 2)


def f_kernel(nt, at_row, more, delays, valid, *refs):
    stream, one, tcos, tsin, two = refs[:5]
    xs, obuf, mbuf, out_sem = refs[-4:]
    stations = stream.shape[0]
    rows = nt * FA
    chunk = FA * LANES
    pitch = xs.shape[0] // stations

    def spread(source, to):
        def one_row(j, _):
            at = pl.multiple_of(j * LANES, LANES)
            xs[pl.ds(to + j, stations, stride=pitch), :] = source[:, pl.ds(at, LANES)].astype(
                f32
            )
            return 0

        count = source.shape[1] // LANES
        lax.fori_loop(0, count, one_row, 0, unroll=16)
        return to + count

    filled = 0
    if more:
        trail, msgs = refs[5], refs[7]
        for source in (stream, trail):
            filled = spread(source, filled)
    else:
        msgs, tail, xin, in_sem = refs[5:9]
        targets = [xin.at[:, pl.ds(i * chunk, chunk)] for i in range(nt)] + [tail]
        copies = [
            pltpu.make_async_copy(stream.at[:, pl.ds(i * chunk, chunk)], target, in_sem.at[i])
            for i, target in enumerate(targets)
        ]
        for copy in copies:
            copy.start()
        for copy, target in zip(copies, targets):
            copy.wait()
            filled = spread(target, filled)
    xs[pl.ds(filled, stations, stride=pitch), :] = jnp.zeros((stations, LANES), f32)
    src = lax.broadcasted_iota(jnp.int32, (2 * LANES, LANES), 0)
    dst = lax.broadcasted_iota(jnp.int32, (2 * LANES, LANES), 1)
    low = lax.broadcasted_iota(jnp.int32, (NQ, LANES), 1) < LO

    def group(g, _):
        blocks = []
        for k in range(GROUP[nt > 1]):
            s = g * GROUP[nt > 1] + k
            shift = delays[s]
            lead = shift // LANES
            within = shift - lead * LANES
            first = xs[pl.ds(s * pitch + lead, rows), :]
            second = xs[pl.ds(s * pitch + lead + 1, rows), :]
            pair = jnp.concatenate([first.astype(bf16), second.astype(bf16)], axis=1)
            move = (src == dst + within).astype(f32).astype(bf16)
            moved = jnp.dot(pair, move, preferred_element_type=f32).astype(bf16)
            blocks += [moved[t * FA : (t + 1) * FA] for t in range(nt)]
        sections = lax.dot_general(
            jnp.concatenate(blocks, axis=1),
            one[...],
            (((0,), (0,)), ((), ())),
            preferred_element_type=f32,
        )
        for k in range(GROUP[nt > 1]):
            s = g * GROUP[nt > 1] + k
            last = (two[...].astype(f32) * valid[s].astype(f32)).astype(bf16)
            for t in range(nt):
                at = (k * nt + t) * FB
                re, im = sections[at : at + FB, :FA], sections[at : at + FB, FA:]
                cosine, sine = tcos[...], tsin[...]
                tr = (re * cosine + im * sine).astype(bf16)
                ti = (im * cosine - re * sine).astype(bf16)
                spec = jnp.dot(
                    last, jnp.concatenate([tr, ti], axis=0), preferred_element_type=f32
                )
                for j in range(FA // LANES):
                    a = spec[:NQ, j * LANES : (j + 1) * LANES]
                    b = spec[NQ:, j * LANES : (j + 1) * LANES]
                    even = jnp.where(low, a, pltpu.roll(b, LO, 1))
                    odd = jnp.where(low, pltpu.roll(a, LO, 1), b)
                    for h, piece in ((2 * j, even), (2 * j + 1, odd)):
                        to = pl.multiple_of(((h * nt + t) * stations + s) * OPITCH, 8)
                        obuf[pl.ds(to, NQ), :] = piece
        return 0

    lax.fori_loop(0, stations // GROUP[nt > 1], group, 0, unroll=UNROLL[nt > 1])

    per = NQ // PIECES
    sent = []
    for i in range(PIECES):

        def gather(q, _):
            for h in range(NHI):
                got = obuf[
                    pl.ds(h * nt * stations * OPITCH + q, nt * stations, stride=OPITCH), :
                ]
                mbuf[q * NHI + h] = got.astype(bf16)
            return 0

        lax.fori_loop(i * per, (i + 1) * per, gather, 0, unroll=4)
        span = pl.ds(i * per * NHI, per * NHI)
        sent.append(
            pltpu.make_async_copy(
                mbuf.at[span], msgs.at[span, pl.ds(at_row, nt * stations), :], out_sem.at[i]
            )
        )
        sent[i].start()
    for copy in sent:
        copy.wait()


def on_chip(value):
    return pltpu.with_memory_space_constraint(value, pltpu.VMEM)


def off_chip(value):
    return pltpu.with_memory_space_constraint(value, pltpu.HBM)


def channelized(stream, delays, valid, tables, so_far=()):
    stations = stream.shape[0]
    smem = pl.BlockSpec(memory_space=pltpu.SMEM)
    vmem = pl.BlockSpec(memory_space=pltpu.VMEM)
    hbm = pl.BlockSpec(memory_space=pltpu.HBM)
    chunk = FA * LANES
    here = stream.shape[1] // chunk
    if so_far:
        msgs, trailing = so_far
        nt, at_row = 1, msgs.shape[1] - stations
        rows = (stream.shape[1] + trailing.shape[1]) // LANES
        stream = on_chip(stream)
        tables = [on_chip(jnp.asarray(table)) for table in tables]
        extra = (on_chip(trailing), off_chip(msgs))
        specs = [smem, smem] + [vmem] * 6 + [hbm]
        outs, out_specs = pltpu.HBM(msgs.shape, bf16), hbm
        aliases = {8: 0}
        buffers = []
    else:
        nt, at_row, extra = here - 1, 0, ()
        stream = off_chip(stream)
        rows = here * FA
        specs = [smem, smem, hbm] + [vmem] * 4
        outs = (
            pltpu.HBM((NQ * NHI, here * stations, LANES), bf16),
            pltpu.VMEM((stations, chunk), bf16),
        )
        out_specs = (hbm, vmem)
        aliases = {}
        buffers = [
            pltpu.VMEM((stations, nt * chunk), bf16),
            pltpu.SemaphoreType.DMA((here,)),
        ]
    pitch = (rows // 16 + 1) * 16 + 8
    return pl.pallas_call(
        lambda *refs: f_kernel(nt, at_row, bool(so_far), *refs),
        out_shape=outs,
        in_specs=specs,
        out_specs=out_specs,
        scratch_shapes=buffers
        + [
            pltpu.VMEM((stations * pitch, LANES), f32),
            pltpu.VMEM((NHI * nt * stations * OPITCH, LANES), f32),
            pltpu.VMEM((NQ * NHI, nt * stations, LANES), bf16),
            pltpu.SemaphoreType.DMA((PIECES,)),
        ],
        input_output_aliases=aliases,
        compiler_params=pltpu.CompilerParams(vmem_limit_bytes=28 << 20),
        name="channelize",
    )(delays, valid, stream, *tables, *extra)


def tone_kernel(tones, msgs, picks):
    stations, count = tones.shape
    sub = lax.broadcasted_iota(jnp.int32, (stations, LANES), 0)
    slot = lax.broadcasted_iota(jnp.int32, (stations, LANES), 1) % NTONE

    def one_tone(k, acc):
        for s in range(stations):
            chan = tones[s, k]
            place = chan // LO
            within = chan - place * LO
            tile = msgs[place].astype(f32)
            total = tile[:stations]
            for t in range(1, tile.shape[0] // stations):
                total = total + tile[t * stations : (t + 1) * stations]
            turned = pltpu.roll(total, (k - within + LANES) % LANES, 1)
            acc = jnp.where((sub == s) & (slot == k), turned, acc)
        return acc

    picks[...] = lax.fori_loop(0, count, one_tone, jnp.zeros((stations, LANES), f32), unroll=2)


def tone_sums(msgs, tone_chan):
    return pl.pallas_call(
        tone_kernel,
        out_shape=jax.ShapeDtypeStruct((tone_chan.shape[0], 2 * NTONE), f32),
        in_specs=[
            pl.BlockSpec(memory_space=pltpu.SMEM),
            pl.BlockSpec(memory_space=pltpu.VMEM),
        ],
        out_specs=pl.BlockSpec(memory_space=pltpu.VMEM),
        compiler_params=pltpu.CompilerParams(vmem_limit_bytes=8 << 20),
        name="tones",
    )(tone_chan, msgs)


PITCH = 136


def x_kernel(norm_scale, per_source, recv, vis, rs, ts, gs):
    sources, rows, _ = recv.shape
    local = per_source
    groups = S // local
    times = sources // groups * rows // local

    def widen(i, _):
        at = pl.multiple_of(i * rows, rows)
        rs[pl.ds(at, rows), :] = recv[i].astype(f32)
        return 0

    lax.fori_loop(0, sources, widen, 0, unroll=8)

    def turn(i, _):
        g = i // local
        s = i - g * local
        got = rs[pl.ds(g * times * local + s, times, stride=local), :]
        ts[pl.ds(pl.multiple_of(i * PITCH, 8), LANES), :] = got.T
        return 0

    lax.fori_loop(0, S, turn, 0, unroll=True)

    lane = lax.broadcasted_iota(jnp.int32, (8, LANES), 1)

    def eight(o, _):
        base = o * 8
        for c in range(8):
            re = ts[pl.ds(base + c, S, stride=PITCH), :]
            im = ts[pl.ds(base + c + LO, S, stride=PITCH), :]
            plus, quad, minus = re.astype(bf16), im.astype(bf16), (-re).astype(bf16)
            straight = jnp.concatenate([plus, quad], axis=1)
            turned = jnp.concatenate([quad, minus], axis=1)
            left = jnp.concatenate([straight, turned], axis=0)
            right = jnp.concatenate([straight, straight], axis=0)
            gram = lax.dot_general(
                left, right, (((1,), (1,)), ((), ())), preferred_element_type=f32
            )
            gs[pl.ds(c * PITCH, 2 * S), :] = gram * norm_scale
        top = pl.multiple_of(base, 8)
        for j in range(S):
            even = gs[pl.ds(2 * j, 8, stride=PITCH), :]
            odd = gs[pl.ds(2 * j + 1, 8, stride=PITCH), :]
            vis[pl.ds(top, 8), pl.ds(j * LANES, LANES)] = jnp.where(lane < S, even, odd)
        return 0

    lax.fori_loop(0, LO // 8, eight, 0, unroll=True)


def correlated(recv, per_source, norm_scale):
    vmem = pl.BlockSpec(memory_space=pltpu.VMEM)
    return pl.pallas_call(
        lambda *refs: x_kernel(norm_scale, per_source, *refs),
        out_shape=jax.ShapeDtypeStruct((LO, 2 * S * S), f32),
        in_specs=[vmem],
        out_specs=vmem,
        scratch_shapes=[
            pltpu.VMEM((recv.shape[0] * recv.shape[1], LANES), f32),
            pltpu.VMEM((S * PITCH, LANES), f32),
            pltpu.VMEM((8 * PITCH, LANES), f32),
        ],
        compiler_params=pltpu.CompilerParams(vmem_limit_bytes=24 << 20),
        name="correlate",
    )(on_chip(recv))


def passed_along(block, axis, distance):
    devices = range(lax.axis_size(axis))
    route = [(i - distance, i) for i in devices if i - distance in devices]
    return lax.ppermute(block, axis, route)


def routed(value, axis, dest):
    return lax.ppermute(value, axis, [(i, dest(i)) for i in range(lax.axis_size(axis))])


def gathered_sum(picks):
    value = picks + routed(picks, "cores", lambda i: i ^ 1)
    value = value + routed(value, "tm", lambda i: i ^ 1)
    size = lax.axis_size("tm")
    half = size // 4
    steps = [
        routed(value, "tm", lambda i, d=d: (i + 2 * (d + half * (i % 2))) % size)
        for d in range(half)
    ]
    value = sum(steps)
    return value + routed(value, "tm", lambda i: i ^ 1)


def shards(samples, delays, valid, tone_chan):
    stations, stretch = samples.shape
    whole = ("stn", "tm", "cores")
    here = stretch // (FA * FB)
    trailing = passed_along(samples[:, :MAXD], ("tm", "cores"), -1)
    own = (delays, valid, make_tables())
    msgs, tail = channelized(samples, *own)
    msgs = channelized(tail, *own, (msgs, trailing))
    spectra_all = here * lax.axis_size("tm") * lax.axis_size("cores")
    norm_scale = 1.0 / math.sqrt(spectra_all)
    recv = lax.all_to_all(msgs, whole, split_axis=0, concat_axis=0, tiled=True)
    phase_cal = gathered_sum(tone_sums(msgs, tone_chan)) * norm_scale
    return (correlated(recv, stations, norm_scale), phase_cal)


def solution(mesh):
    return jax.shard_map(
        shards,
        mesh=mesh,
        in_specs=(P("stn", ("tm", "cores")), P("stn"), P("stn"), P("stn", None)),
        out_specs=(P(("stn", "tm", "cores"), None), P("stn", None)),
        check_vma=False,
    )
```

```python
import math

import jax
import jax.numpy as jnp
import ml_dtypes
import numpy as np
from jax import lax
from jax.experimental import pallas as pl
from jax.experimental.pallas import tpu as pltpu
from jax.sharding import PartitionSpec as P

S = 64
NCH = 16384
FA = 256
FB = 128
NTONE = 64
MAXD = 32768
NQ = FB // 2
NHI = 4
LO = FA // NHI
LANES = 128

f32 = jnp.float32
bf16 = jnp.bfloat16


def make_tables():
    k1 = np.arange(FA)
    angles = 2.0 * np.pi / FA * (k1[:, None] * k1[None, :] % FA)
    section_one = np.concatenate([np.cos(angles), -np.sin(angles)], axis=1).astype(
        ml_dtypes.bfloat16
    )
    n2 = np.arange(FB)
    length = FA * FB
    twists = 2.0 * np.pi / length * (n2[:, None] * k1[None, :] % length)
    scale = 1.0 / math.sqrt(length)
    twist_cos = (np.cos(twists) * scale).astype(np.float32)
    twist_sin = (np.sin(twists) * scale).astype(np.float32)
    q = np.arange(NQ)
    thetas = 2.0 * np.pi / FB * (q[:, None] * n2[None, :] % FB)
    cosine, sine = np.cos(thetas), np.sin(thetas)
    section_two = np.block([[cosine, sine], [-sine, cosine]]).astype(ml_dtypes.bfloat16)
    return (section_one, twist_cos, twist_sin, section_two)


OPITCH = NQ + 8
PIECES = 4
GROUP = (8, 2)
UNROLL = (1, 2)


def f_kernel(nt, skip, at_row, more, *refs):
    sources, refs = refs[:7], refs[7:]
    trail = refs[0] if more else None
    msgs = refs[2 if more else 0]
    delays, valid, one, tcos, tsin, two, xin, xs, obuf, mbuf, small_sem, in_sem, out_sem = refs[
        -13:
    ]
    stream = sources[0]
    small = [
        pltpu.make_async_copy(source, target, small_sem.at[i])
        for i, (source, target) in enumerate(
            zip(sources[1:], (delays, valid, one, tcos, tsin, two))
        )
    ]
    stations = stream.shape[0]
    rows = nt * FA
    chunk = FA * LANES
    pitch = xs.shape[0] // stations
    copies = [
        pltpu.make_async_copy(
            stream.at[:, pl.ds(skip + i * chunk, chunk)],
            xin.at[:, pl.ds(i * chunk, chunk)],
            in_sem.at[i],
        )
        for i in range(xin.shape[1] // chunk)
    ]
    for copy in copies + small:
        copy.start()

    def spread(source, base, to):
        def one_row(j, _):
            at = pl.multiple_of((base + j) * LANES, LANES)
            xs[pl.ds(to + j, stations, stride=pitch), :] = source[:, pl.ds(at, LANES)].astype(
                f32
            )
            return 0

        lax.fori_loop(0, FA, one_row, 0, unroll=16)

    filled = len(copies) * FA
    if more:
        spread(trail, 0, filled)
    for i, copy in enumerate(copies):
        copy.wait()
        spread(xin, i * FA, i * FA)
    if more:
        filled += FA
    xs[pl.ds(filled, stations, stride=pitch), :] = jnp.zeros((stations, LANES), f32)
    for copy in small:
        copy.wait()
    src = lax.broadcasted_iota(jnp.int32, (2 * LANES, LANES), 0)
    dst = lax.broadcasted_iota(jnp.int32, (2 * LANES, LANES), 1)
    low = lax.broadcasted_iota(jnp.int32, (NQ, LANES), 1) < LO

    def group(g, _):
        blocks = []
        for k in range(GROUP[nt > 1]):
            s = g * GROUP[nt > 1] + k
            shift = delays[s]
            lead = shift // LANES
            within = shift - lead * LANES
            first = xs[pl.ds(s * pitch + lead, rows), :]
            second = xs[pl.ds(s * pitch + lead + 1, rows), :]
            pair = jnp.concatenate([first.astype(bf16), second.astype(bf16)], axis=1)
            move = (src == dst + within).astype(f32).astype(bf16)
            moved = jnp.dot(pair, move, preferred_element_type=f32).astype(bf16)
            blocks += [moved[t * FA : (t + 1) * FA] for t in range(nt)]
        sections = lax.dot_general(
            jnp.concatenate(blocks, axis=1),
            one[...],
            (((0,), (0,)), ((), ())),
            preferred_element_type=f32,
        )
        for k in range(GROUP[nt > 1]):
            s = g * GROUP[nt > 1] + k
            last = (two[...].astype(f32) * valid[s].astype(f32)).astype(bf16)
            for t in range(nt):
                at = (k * nt + t) * FB
                re, im = sections[at : at + FB, :FA], sections[at : at + FB, FA:]
                cosine, sine = tcos[...], tsin[...]
                tr = (re * cosine + im * sine).astype(bf16)
                ti = (im * cosine - re * sine).astype(bf16)
                spec = jnp.dot(
                    last, jnp.concatenate([tr, ti], axis=0), preferred_element_type=f32
                )
                for j in range(FA // LANES):
                    a = spec[:NQ, j * LANES : (j + 1) * LANES]
                    b = spec[NQ:, j * LANES : (j + 1) * LANES]
                    even = jnp.where(low, a, pltpu.roll(b, LO, 1))
                    odd = jnp.where(low, pltpu.roll(a, LO, 1), b)
                    for h, piece in ((2 * j, even), (2 * j + 1, odd)):
                        to = pl.multiple_of(((h * nt + t) * stations + s) * OPITCH, 8)
                        obuf[pl.ds(to, NQ), :] = piece
        return 0

    lax.fori_loop(0, stations // GROUP[nt > 1], group, 0, unroll=UNROLL[nt > 1])

    per = NQ // PIECES
    sent = []
    for i in range(PIECES):

        def gather(q, _):
            for h in range(NHI):
                got = obuf[
                    pl.ds(h * nt * stations * OPITCH + q, nt * stations, stride=OPITCH), :
                ]
                mbuf[q * NHI + h] = got.astype(bf16)
            return 0

        lax.fori_loop(i * per, (i + 1) * per, gather, 0, unroll=4)
        span = pl.ds(i * per * NHI, per * NHI)
        sent.append(
            pltpu.make_async_copy(
                mbuf.at[span], msgs.at[span, pl.ds(at_row, nt * stations), :], out_sem.at[i]
            )
        )
        sent[i].start()
    for copy in sent:
        copy.wait()


def on_chip(value):
    return pltpu.with_memory_space_constraint(value, pltpu.VMEM)


def off_chip(value):
    return pltpu.with_memory_space_constraint(value, pltpu.HBM)


def channelized(stream, delays, valid, tables, so_far=()):
    stations = stream.shape[0]
    hbm = pl.BlockSpec(memory_space=pl.ANY)
    vmem = pl.BlockSpec(memory_space=pltpu.VMEM)
    chunk = FA * LANES
    here = stream.shape[1] // chunk
    specs = [pl.BlockSpec(memory_space=pltpu.HBM)] * 7
    if so_far:
        msgs, trailing = so_far
        nt, skip, at_row = 1, (here - 1) * chunk, (here - 1) * stations
        extra = (on_chip(trailing), msgs)
        specs += [vmem, hbm]
        aliases = {8: 0}
        held = 1
    else:
        nt, skip, at_row, extra = here - 1, 0, 0, ()
        aliases = {}
        held = here
    pitch = ((held + len(aliases)) * FA // 16 + 1) * 16 + 8
    return pl.pallas_call(
        lambda *refs: f_kernel(nt, skip, at_row, bool(so_far), *refs),
        out_shape=jax.ShapeDtypeStruct((NQ * NHI, here * stations, LANES), bf16),
        in_specs=specs,
        out_specs=hbm,
        scratch_shapes=[
            pltpu.SMEM(delays.shape, delays.dtype),
            pltpu.SMEM(valid.shape, valid.dtype),
        ]
        + [pltpu.VMEM(table.shape, table.dtype) for table in tables]
        + [
            pltpu.VMEM((stations, held * chunk), bf16),
            pltpu.VMEM((stations * pitch, LANES), f32),
            pltpu.VMEM((NHI * nt * stations * OPITCH, LANES), f32),
            pltpu.VMEM((NQ * NHI, nt * stations, LANES), bf16),
            pltpu.SemaphoreType.DMA((2 + len(tables),)),
            pltpu.SemaphoreType.DMA((held,)),
            pltpu.SemaphoreType.DMA((PIECES,)),
        ],
        input_output_aliases=aliases,
        compiler_params=pltpu.CompilerParams(vmem_limit_bytes=28 << 20),
        name="channelize",
    )(*[off_chip(jnp.asarray(value)) for value in (stream, delays, valid, *tables)], *extra)


def tone_kernel(tones, msgs, picks):
    stations, count = tones.shape
    sub = lax.broadcasted_iota(jnp.int32, (stations, LANES), 0)
    slot = lax.broadcasted_iota(jnp.int32, (stations, LANES), 1) % NTONE

    def one_tone(k, acc):
        for s in range(stations):
            chan = tones[s, k]
            place = chan // LO
            within = chan - place * LO
            tile = msgs[place].astype(f32)
            total = tile[:stations]
            for t in range(1, tile.shape[0] // stations):
                total = total + tile[t * stations : (t + 1) * stations]
            turned = pltpu.roll(total, (k - within + LANES) % LANES, 1)
            acc = jnp.where((sub == s) & (slot == k), turned, acc)
        return acc

    picks[...] = lax.fori_loop(0, count, one_tone, jnp.zeros((stations, LANES), f32), unroll=2)


def tone_sums(msgs, tone_chan):
    return pl.pallas_call(
        tone_kernel,
        out_shape=jax.ShapeDtypeStruct((tone_chan.shape[0], 2 * NTONE), f32),
        in_specs=[
            pl.BlockSpec(memory_space=pltpu.SMEM),
            pl.BlockSpec(memory_space=pltpu.VMEM),
        ],
        out_specs=pl.BlockSpec(memory_space=pltpu.VMEM),
        compiler_params=pltpu.CompilerParams(vmem_limit_bytes=8 << 20),
        name="tones",
    )(tone_chan, msgs)


PITCH = 136


def x_kernel(norm_scale, per_source, recv, vis, rs, ts, gs, block, out_sem):
    sources, rows, _ = recv.shape
    local = per_source
    groups = S // local
    times = sources // groups * rows // local

    def widen(i, _):
        at = pl.multiple_of(i * rows, rows)
        rs[pl.ds(at, rows), :] = recv[i].astype(f32)
        return 0

    lax.fori_loop(0, sources, widen, 0, unroll=8)

    def turn(i, _):
        g = i // local
        s = i - g * local
        got = rs[pl.ds(g * times * local + s, times, stride=local), :]
        ts[pl.ds(pl.multiple_of(i * PITCH, 8), LANES), :] = got.T
        return 0

    lax.fori_loop(0, S, turn, 0, unroll=True)

    lane = lax.broadcasted_iota(jnp.int32, (8, LANES), 1)

    sent = []

    def eight(o, _):
        base = o * 8
        for c in range(8):
            re = ts[pl.ds(base + c, S, stride=PITCH), :]
            im = ts[pl.ds(base + c + LO, S, stride=PITCH), :]
            plus, quad, minus = re.astype(bf16), im.astype(bf16), (-re).astype(bf16)
            straight = jnp.concatenate([plus, quad], axis=1)
            turned = jnp.concatenate([quad, minus], axis=1)
            left = jnp.concatenate([straight, turned], axis=0)
            right = jnp.concatenate([straight, straight], axis=0)
            gram = lax.dot_general(
                left, right, (((1,), (1,)), ((), ())), preferred_element_type=f32
            )
            gs[pl.ds(c * PITCH, 2 * S), :] = gram * norm_scale
        top = base
        for j in range(S):
            even = gs[pl.ds(2 * j, 8, stride=PITCH), :]
            odd = gs[pl.ds(2 * j + 1, 8, stride=PITCH), :]
            block[pl.ds(top, 8), pl.ds(j * LANES, LANES)] = jnp.where(lane < S, even, odd)
        return 0

    for o in range(LO // 8):
        eight(o, 0)
        sent.append(
            pltpu.make_async_copy(
                block.at[pl.ds(o * 8, 8), :], vis.at[pl.ds(o * 8, 8), :], out_sem.at[o]
            )
        )
        sent[o].start()
    for copy in sent:
        copy.wait()


def correlated(recv, per_source, norm_scale):
    vmem = pl.BlockSpec(memory_space=pltpu.VMEM)
    return pl.pallas_call(
        lambda *refs: x_kernel(norm_scale, per_source, *refs),
        out_shape=jax.ShapeDtypeStruct((LO, 2 * S * S), f32),
        in_specs=[vmem],
        out_specs=pl.BlockSpec(memory_space=pl.ANY),
        scratch_shapes=[
            pltpu.VMEM((recv.shape[0] * recv.shape[1], LANES), f32),
            pltpu.VMEM((S * PITCH, LANES), f32),
            pltpu.VMEM((8 * PITCH, LANES), f32),
            pltpu.VMEM((LO, 2 * S * S), f32),
            pltpu.SemaphoreType.DMA((LO // 8,)),
        ],
        compiler_params=pltpu.CompilerParams(vmem_limit_bytes=24 << 20),
        name="correlate",
    )(on_chip(recv))


def passed_along(block, axis, distance):
    devices = range(lax.axis_size(axis))
    route = [(i - distance, i) for i in devices if i - distance in devices]
    return lax.ppermute(block, axis, route)


def routed(value, axis, dest):
    return lax.ppermute(value, axis, [(i, dest(i)) for i in range(lax.axis_size(axis))])


def gathered_sum(picks):
    value = picks + routed(picks, "cores", lambda i: i ^ 1)
    value = value + routed(value, "tm", lambda i: i ^ 1)
    size = lax.axis_size("tm")
    half = size // 4
    steps = [
        routed(value, "tm", lambda i, d=d: (i + 2 * (d + half * (i % 2))) % size)
        for d in range(half)
    ]
    value = sum(steps)
    return value + routed(value, "tm", lambda i: i ^ 1)


def shards(samples, delays, valid, tone_chan):
    stations, stretch = samples.shape
    whole = ("stn", "tm", "cores")
    here = stretch // (FA * FB)
    trailing = passed_along(samples[:, :MAXD], ("tm", "cores"), -1)
    own = (samples, delays, valid, make_tables())
    msgs = channelized(*own, (channelized(*own), trailing))
    spectra_all = here * lax.axis_size("tm") * lax.axis_size("cores")
    norm_scale = 1.0 / math.sqrt(spectra_all)
    recv = lax.all_to_all(msgs, whole, split_axis=0, concat_axis=0, tiled=True)
    phase_cal = gathered_sum(tone_sums(msgs, tone_chan)) * norm_scale
    return (correlated(recv, stations, norm_scale), phase_cal)


def solution(mesh):
    return jax.shard_map(
        shards,
        mesh=mesh,
        in_specs=(P("stn", ("tm", "cores")), P("stn"), P("stn"), P("stn", None)),
        out_specs=(P(("stn", "tm", "cores"), None), P("stn", None)),
        check_vma=False,
    )
```

```python
import math

import jax
import jax.numpy as jnp
import ml_dtypes
import numpy as np
from jax import lax
from jax.experimental import pallas as pl
from jax.experimental.pallas import tpu as pltpu
from jax.sharding import PartitionSpec as P

S = 64
NCH = 16384
FA = 256
FB = 128
NTONE = 64
MAXD = 32768
NQ = FB // 2
NHI = 4
LO = FA // NHI
LANES = 128

f32 = jnp.float32
bf16 = jnp.bfloat16


def make_tables():
    k1 = np.arange(FA)
    angles = 2.0 * np.pi / FA * (k1[:, None] * k1[None, :] % FA)
    section_one = np.concatenate([np.cos(angles), -np.sin(angles)], axis=1).astype(
        ml_dtypes.bfloat16
    )
    n2 = np.arange(FB)
    length = FA * FB
    twists = 2.0 * np.pi / length * (n2[:, None] * k1[None, :] % length)
    scale = 1.0 / math.sqrt(length)
    twist_cos = (np.cos(twists) * scale).astype(np.float32)
    twist_sin = (np.sin(twists) * scale).astype(np.float32)
    q = np.arange(NQ)
    thetas = 2.0 * np.pi / FB * (q[:, None] * n2[None, :] % FB)
    cosine, sine = np.cos(thetas), np.sin(thetas)
    section_two = np.block([[cosine, sine], [-sine, cosine]]).astype(ml_dtypes.bfloat16)
    return (section_one, twist_cos, twist_sin, section_two)


OPITCH = NQ + 8
PIECES = 4
GROUP = (8, 2)
UNROLL = (1, 2)


def f_kernel(nt, skip, at_row, more, *refs):
    stream, refs, given = refs[0], refs[7:], refs[1:7]
    trail = refs[0] if more else None
    msgs = refs[2 if more else 0]
    xin, xs, obuf, mbuf, in_sem, out_sem, small_sem = refs[-13:-6]
    held = refs[-6:]
    if more:
        given, held, tables = given[:2], held[:2], given[2:]
    else:
        tables = held[2:]
    delays, valid = held[:2]
    one, tcos, tsin, two = tables
    small = [
        pltpu.make_async_copy(source, target, small_sem.at[i])
        for i, (source, target) in enumerate(zip(given, held))
    ]
    stations = stream.shape[0]
    rows = nt * FA
    chunk = FA * LANES
    pitch = xs.shape[0] // stations
    copies = [
        pltpu.make_async_copy(
            stream.at[:, pl.ds(skip + i * chunk, chunk)],
            xin.at[:, pl.ds(i * chunk, chunk)],
            in_sem.at[i],
        )
        for i in range(xin.shape[1] // chunk)
    ]
    for copy in copies + small:
        copy.start()

    def spread(source, base, to):
        def one_row(j, _):
            at = pl.multiple_of((base + j) * LANES, LANES)
            xs[pl.ds(to + j, stations, stride=pitch), :] = source[:, pl.ds(at, LANES)].astype(
                f32
            )
            return 0

        lax.fori_loop(0, FA, one_row, 0, unroll=16)

    filled = len(copies) * FA
    if more:
        spread(trail, 0, filled)
    for i, copy in enumerate(copies):
        copy.wait()
        spread(xin, i * FA, i * FA)
    if more:
        filled += FA
    xs[pl.ds(filled, stations, stride=pitch), :] = jnp.zeros((stations, LANES), f32)
    for copy in small:
        copy.wait()
    src = lax.broadcasted_iota(jnp.int32, (2 * LANES, LANES), 0)
    dst = lax.broadcasted_iota(jnp.int32, (2 * LANES, LANES), 1)
    low = lax.broadcasted_iota(jnp.int32, (NQ, LANES), 1) < LO

    def group(g, _):
        blocks = []
        for k in range(GROUP[nt > 1]):
            s = g * GROUP[nt > 1] + k
            shift = delays[s]
            lead = shift // LANES
            within = shift - lead * LANES
            first = xs[pl.ds(s * pitch + lead, rows), :]
            second = xs[pl.ds(s * pitch + lead + 1, rows), :]
            pair = jnp.concatenate([first.astype(bf16), second.astype(bf16)], axis=1)
            move = (src == dst + within).astype(f32).astype(bf16)
            moved = jnp.dot(pair, move, preferred_element_type=f32).astype(bf16)
            blocks += [moved[t * FA : (t + 1) * FA] for t in range(nt)]
        sections = lax.dot_general(
            jnp.concatenate(blocks, axis=1),
            one[...],
            (((0,), (0,)), ((), ())),
            preferred_element_type=f32,
        )
        for k in range(GROUP[nt > 1]):
            s = g * GROUP[nt > 1] + k
            last = (two[...].astype(f32) * valid[s].astype(f32)).astype(bf16)
            for t in range(nt):
                at = (k * nt + t) * FB
                re, im = sections[at : at + FB, :FA], sections[at : at + FB, FA:]
                cosine, sine = tcos[...], tsin[...]
                tr = (re * cosine + im * sine).astype(bf16)
                ti = (im * cosine - re * sine).astype(bf16)
                spec = jnp.dot(
                    last, jnp.concatenate([tr, ti], axis=0), preferred_element_type=f32
                )
                for j in range(FA // LANES):
                    a = spec[:NQ, j * LANES : (j + 1) * LANES]
                    b = spec[NQ:, j * LANES : (j + 1) * LANES]
                    even = jnp.where(low, a, pltpu.roll(b, LO, 1))
                    odd = jnp.where(low, pltpu.roll(a, LO, 1), b)
                    for h, piece in ((2 * j, even), (2 * j + 1, odd)):
                        to = pl.multiple_of(((h * nt + t) * stations + s) * OPITCH, 8)
                        obuf[pl.ds(to, NQ), :] = piece
        return 0

    lax.fori_loop(0, stations // GROUP[nt > 1], group, 0, unroll=UNROLL[nt > 1])

    per = NQ // PIECES
    sent = []
    for i in range(PIECES):

        def gather(q, _):
            for h in range(NHI):
                got = obuf[
                    pl.ds(h * nt * stations * OPITCH + q, nt * stations, stride=OPITCH), :
                ]
                mbuf[q * NHI + h] = got.astype(bf16)
            return 0

        lax.fori_loop(i * per, (i + 1) * per, gather, 0, unroll=4)
        span = pl.ds(i * per * NHI, per * NHI)
        sent.append(
            pltpu.make_async_copy(
                mbuf.at[span], msgs.at[span, pl.ds(at_row, nt * stations), :], out_sem.at[i]
            )
        )
        sent[i].start()
    for copy in sent:
        copy.wait()


def on_chip(value):
    return pltpu.with_memory_space_constraint(value, pltpu.VMEM)


def off_chip(value):
    return pltpu.with_memory_space_constraint(value, pltpu.HBM)


def channelized(stream, delays, valid, tables, so_far=()):
    stations = stream.shape[0]
    hbm = pl.BlockSpec(memory_space=pl.ANY)
    vmem = pl.BlockSpec(memory_space=pltpu.VMEM)
    chunk = FA * LANES
    here = stream.shape[1] // chunk
    far = pl.BlockSpec(memory_space=pltpu.HBM)
    tables = [jnp.asarray(table) for table in tables]
    if so_far:
        msgs, trailing = so_far
        nt, skip, at_row = 1, (here - 1) * chunk, (here - 1) * stations
        extra = (on_chip(trailing), msgs)
        specs = [far] * 3 + [vmem] * 5 + [hbm]
        tables = [on_chip(table) for table in tables]
        aliases = {8: 0}
        held = 1
    else:
        nt, skip, at_row, extra = here - 1, 0, 0, ()
        aliases = {}
        held = here
        specs = [far] * 7
        tables = [off_chip(table) for table in tables]
    pitch = ((held + len(aliases)) * FA // 16 + 1) * 16 + 8
    return pl.pallas_call(
        lambda *refs: f_kernel(nt, skip, at_row, bool(so_far), *refs),
        out_shape=jax.ShapeDtypeStruct((NQ * NHI, here * stations, LANES), bf16),
        in_specs=specs,
        out_specs=hbm,
        scratch_shapes=[
            pltpu.VMEM((stations, held * chunk), bf16),
            pltpu.VMEM((stations * pitch, LANES), f32),
            pltpu.VMEM((NHI * nt * stations * OPITCH, LANES), f32),
            pltpu.VMEM((NQ * NHI, nt * stations, LANES), bf16),
            pltpu.SemaphoreType.DMA((held,)),
            pltpu.SemaphoreType.DMA((PIECES,)),
            pltpu.SemaphoreType.DMA((2 + len(tables),)),
            pltpu.SMEM(delays.shape, delays.dtype),
            pltpu.SMEM(valid.shape, valid.dtype),
        ]
        + [pltpu.VMEM(table.shape, table.dtype) for table in tables],
        input_output_aliases=aliases,
        compiler_params=pltpu.CompilerParams(vmem_limit_bytes=28 << 20),
        name="channelize",
    )(*[off_chip(value) for value in (stream, delays, valid)], *tables, *extra)


def tone_kernel(tones, msgs, picks, sums):
    stations, count = tones.shape
    places, rows, _ = msgs.shape

    def add_times(p, _):
        tile = msgs[p].astype(f32)
        total = tile[:stations]
        for t in range(1, rows // stations):
            total = total + tile[t * stations : (t + 1) * stations]
        sums[pl.ds(pl.multiple_of(p * stations, stations), stations), :] = total
        return 0

    lax.fori_loop(0, places, add_times, 0, unroll=8)
    sub = lax.broadcasted_iota(jnp.int32, (stations, LANES), 0)
    slot = lax.broadcasted_iota(jnp.int32, (stations, LANES), 1) % NTONE

    def one_tone(k, acc):
        here = jnp.where(slot == k, sub, -1)
        for s in range(stations):
            chan = tones[s, k]
            place = lax.shift_right_logical(chan, LO.bit_length() - 1)
            within = lax.bitwise_and(chan, LO - 1)
            total = sums[pl.ds(pl.multiple_of(place * stations, stations), stations), :]
            turned = pltpu.roll(total, lax.bitwise_and(k - within, LANES - 1), 1)
            acc = jnp.where(here == s, turned, acc)
        return acc

    picks[...] = lax.fori_loop(0, count, one_tone, jnp.zeros((stations, LANES), f32), unroll=4)


def tone_sums(msgs, tone_chan):
    return pl.pallas_call(
        tone_kernel,
        out_shape=jax.ShapeDtypeStruct((tone_chan.shape[0], 2 * NTONE), f32),
        in_specs=[
            pl.BlockSpec(memory_space=pltpu.SMEM),
            pl.BlockSpec(memory_space=pltpu.VMEM),
        ],
        out_specs=pl.BlockSpec(memory_space=pltpu.VMEM),
        scratch_shapes=[pltpu.VMEM((msgs.shape[0] * tone_chan.shape[0], LANES), f32)],
        compiler_params=pltpu.CompilerParams(vmem_limit_bytes=8 << 20),
        name="tones",
    )(tone_chan, msgs)


PITCH = 136


def x_kernel(norm_scale, per_source, recv, vis, rs, ts, gs, block, out_sem):
    sources, rows, _ = recv.shape
    local = per_source
    groups = S // local
    times = sources // groups * rows // local

    def widen(i, _):
        at = pl.multiple_of(i * rows, rows)
        rs[pl.ds(at, rows), :] = recv[i].astype(f32)
        return 0

    lax.fori_loop(0, sources, widen, 0, unroll=8)

    def turn(i, _):
        g = i // local
        s = i - g * local
        got = rs[pl.ds(g * times * local + s, times, stride=local), :]
        ts[pl.ds(pl.multiple_of(i * PITCH, 8), LANES), :] = got.T
        return 0

    lax.fori_loop(0, S, turn, 0, unroll=True)

    lane = lax.broadcasted_iota(jnp.int32, (8, LANES), 1)

    sent = []

    def eight(o, _):
        base = o * 8
        for c in range(8):
            re = ts[pl.ds(base + c, S, stride=PITCH), :]
            im = ts[pl.ds(base + c + LO, S, stride=PITCH), :]
            plus, quad, minus = re.astype(bf16), im.astype(bf16), (-re).astype(bf16)
            straight = jnp.concatenate([plus, quad], axis=1)
            turned = jnp.concatenate([quad, minus], axis=1)
            left = jnp.concatenate([straight, turned], axis=0)
            right = jnp.concatenate([straight, straight], axis=0)
            gram = lax.dot_general(
                left, right, (((1,), (1,)), ((), ())), preferred_element_type=f32
            )
            gs[pl.ds(c * PITCH, 2 * S), :] = gram * norm_scale
        top = base
        for j in range(S):
            even = gs[pl.ds(2 * j, 8, stride=PITCH), :]
            odd = gs[pl.ds(2 * j + 1, 8, stride=PITCH), :]
            block[pl.ds(top, 8), pl.ds(j * LANES, LANES)] = jnp.where(lane < S, even, odd)
        return 0

    for o in range(LO // 8):
        eight(o, 0)
        sent.append(
            pltpu.make_async_copy(
                block.at[pl.ds(o * 8, 8), :], vis.at[pl.ds(o * 8, 8), :], out_sem.at[o]
            )
        )
        sent[o].start()
    for copy in sent:
        copy.wait()


def correlated(recv, per_source, norm_scale):
    vmem = pl.BlockSpec(memory_space=pltpu.VMEM)
    return pl.pallas_call(
        lambda *refs: x_kernel(norm_scale, per_source, *refs),
        out_shape=jax.ShapeDtypeStruct((LO, 2 * S * S), f32),
        in_specs=[vmem],
        out_specs=pl.BlockSpec(memory_space=pl.ANY),
        scratch_shapes=[
            pltpu.VMEM((recv.shape[0] * recv.shape[1], LANES), f32),
            pltpu.VMEM((S * PITCH, LANES), f32),
            pltpu.VMEM((8 * PITCH, LANES), f32),
            pltpu.VMEM((LO, 2 * S * S), f32),
            pltpu.SemaphoreType.DMA((LO // 8,)),
        ],
        compiler_params=pltpu.CompilerParams(vmem_limit_bytes=24 << 20),
        name="correlate",
    )(on_chip(recv))


def passed_along(block, axis, distance):
    devices = range(lax.axis_size(axis))
    route = [(i - distance, i) for i in devices if i - distance in devices]
    return lax.ppermute(block, axis, route)


def routed(value, axis, dest):
    return lax.ppermute(value, axis, [(i, dest(i)) for i in range(lax.axis_size(axis))])


def gathered_sum(picks):
    value = picks + routed(picks, "cores", lambda i: i ^ 1)
    value = value + routed(value, "tm", lambda i: i ^ 1)
    size = lax.axis_size("tm")
    half = size // 4
    steps = [
        routed(value, "tm", lambda i, d=d: (i + 2 * (d + half * (i % 2))) % size)
        for d in range(half)
    ]
    value = sum(steps)
    return value + routed(value, "tm", lambda i: i ^ 1)


def shards(samples, delays, valid, tone_chan):
    stations, stretch = samples.shape
    whole = ("stn", "tm", "cores")
    here = stretch // (FA * FB)
    trailing = passed_along(samples[:, :MAXD], ("tm", "cores"), -1)
    own = (samples, delays, valid, make_tables())
    msgs = channelized(*own, (channelized(*own), trailing))
    spectra_all = here * lax.axis_size("tm") * lax.axis_size("cores")
    norm_scale = 1.0 / math.sqrt(spectra_all)
    recv = lax.all_to_all(msgs, whole, split_axis=0, concat_axis=0, tiled=True)
    phase_cal = gathered_sum(tone_sums(msgs, tone_chan)) * norm_scale
    return (correlated(recv, stations, norm_scale), phase_cal)


def solution(mesh):
    return jax.shard_map(
        shards,
        mesh=mesh,
        in_specs=(P("stn", ("tm", "cores")), P("stn"), P("stn"), P("stn", None)),
        out_specs=(P(("stn", "tm", "cores"), None), P("stn", None)),
        check_vma=False,
    )
```

```python
import math

import jax
import jax.numpy as jnp
import ml_dtypes
import numpy as np
from jax import lax
from jax.experimental import pallas as pl
from jax.experimental.pallas import tpu as pltpu
from jax.sharding import PartitionSpec as P

S = 64
NCH = 16384
FA = 256
FB = 128
NTONE = 64
MAXD = 32768
NQ = FB // 2
NHI = 4
LO = FA // NHI
LANES = 128

f32 = jnp.float32
bf16 = jnp.bfloat16


def make_tables():
    k1 = np.arange(FA)
    angles = 2.0 * np.pi / FA * (k1[:, None] * k1[None, :] % FA)
    section_one = np.concatenate([np.cos(angles), -np.sin(angles)], axis=1).astype(
        ml_dtypes.bfloat16
    )
    n2 = np.arange(FB)
    length = FA * FB
    twists = 2.0 * np.pi / length * (n2[:, None] * k1[None, :] % length)
    scale = 1.0 / math.sqrt(length)
    twist_cos = (np.cos(twists) * scale).astype(np.float32)
    twist_sin = (np.sin(twists) * scale).astype(np.float32)
    q = np.arange(NQ)
    thetas = 2.0 * np.pi / FB * (q[:, None] * n2[None, :] % FB)
    cosine, sine = np.cos(thetas), np.sin(thetas)
    section_two = np.block([[cosine, sine], [-sine, cosine]]).astype(ml_dtypes.bfloat16)
    return (section_one, twist_cos, twist_sin, section_two)


OPITCH = NQ + 8
PIECES = 4
HALVES = 2
ROWS = MAXD // LANES


def on_chip(value):
    return pltpu.with_memory_space_constraint(value, pltpu.VMEM)


def off_chip(value):
    return pltpu.with_memory_space_constraint(value, pltpu.HBM)


def spread(source, base, xs, first, stride):
    def one_row(j, _):
        at = pl.multiple_of((base + j) * LANES, LANES)
        xs[pl.ds(first + j, source.shape[0], stride=stride), :] = source[
            :, pl.ds(at, LANES)
        ].astype(f32)
        return 0

    lax.fori_loop(0, FA, one_row, 0, unroll=16)


def transform(chosen, nt, stations, delays, valid, tables, xs, obuf):
    one, tcos, tsin, two = tables
    rows = nt * FA
    pitch = xs.shape[0] // stations
    src = lax.broadcasted_iota(jnp.int32, (2 * LANES, LANES), 0)
    dst = lax.broadcasted_iota(jnp.int32, (2 * LANES, LANES), 1)
    low = lax.broadcasted_iota(jnp.int32, (NQ, LANES), 1) < LO
    blocks = []
    for s in chosen:
        shift = delays[s]
        lead = shift // LANES
        within = shift - lead * LANES
        first = xs[pl.ds(s * pitch + lead, rows), :]
        second = xs[pl.ds(s * pitch + lead + 1, rows), :]
        pair = jnp.concatenate([first.astype(bf16), second.astype(bf16)], axis=1)
        move = (src == dst + within).astype(f32).astype(bf16)
        moved = jnp.dot(pair, move, preferred_element_type=f32).astype(bf16)
        blocks += [moved[t * FA : (t + 1) * FA] for t in range(nt)]
    sections = lax.dot_general(
        jnp.concatenate(blocks, axis=1),
        one[...],
        (((0,), (0,)), ((), ())),
        preferred_element_type=f32,
    )
    for k, s in enumerate(chosen):
        last = (two[...].astype(f32) * valid[s].astype(f32)).astype(bf16)
        for t in range(nt):
            at = (k * nt + t) * FB
            re, im = sections[at : at + FB, :FA], sections[at : at + FB, FA:]
            cosine, sine = tcos[...], tsin[...]
            tr = (re * cosine + im * sine).astype(bf16)
            ti = (im * cosine - re * sine).astype(bf16)
            spec = jnp.dot(last, jnp.concatenate([tr, ti], axis=0), preferred_element_type=f32)
            for j in range(FA // LANES):
                a = spec[:NQ, j * LANES : (j + 1) * LANES]
                b = spec[NQ:, j * LANES : (j + 1) * LANES]
                even = jnp.where(low, a, pltpu.roll(b, LO, 1))
                odd = jnp.where(low, pltpu.roll(a, LO, 1), b)
                for h, piece in ((2 * j, even), (2 * j + 1, odd)):
                    to = ((h * nt + t) * stations + s) * OPITCH
                    obuf[pl.ds(pl.multiple_of(to, 8), NQ), :] = piece


def write_messages(nt, at_row, stations, obuf, mbuf, msgs, out_sem):
    per = NQ // PIECES
    sent = []
    for i in range(PIECES):

        def gather(q, _):
            for h in range(NHI):
                got = obuf[
                    pl.ds(h * nt * stations * OPITCH + q, nt * stations, stride=OPITCH), :
                ]
                mbuf[q * NHI + h] = got.astype(bf16)
            return 0

        lax.fori_loop(i * per, (i + 1) * per, gather, 0, unroll=4)
        span = pl.ds(i * per * NHI, per * NHI)
        sent.append(
            pltpu.make_async_copy(
                mbuf.at[span], msgs.at[span, pl.ds(at_row, nt * stations), :], out_sem.at[i]
            )
        )
        sent[i].start()
    for copy in sent:
        copy.wait()


def early_kernel(nt, *refs):
    stream, given, msgs = refs[0], refs[1:7], refs[7]
    xin, xs, obuf, mbuf, in_sem, out_sem, small_sem = refs[8:15]
    held = refs[15:]
    stations = stream.shape[0]
    chunk = FA * LANES
    pitch = xs.shape[0] // stations
    copies = [
        pltpu.make_async_copy(
            stream.at[:, pl.ds(i * chunk, chunk)],
            xin.at[:, pl.ds(i * chunk, chunk)],
            in_sem.at[i],
        )
        for i in range(nt + 1)
    ]
    small = [
        pltpu.make_async_copy(source, target, small_sem.at[i])
        for i, (source, target) in enumerate(zip(given, held))
    ]
    for copy in copies + small:
        copy.start()
    for i, copy in enumerate(copies):
        copy.wait()
        spread(xin, i * FA, xs, i * FA, pitch)
    xs[pl.ds((nt + 1) * FA, stations, stride=pitch), :] = jnp.zeros((stations, LANES), f32)
    for copy in small:
        copy.wait()

    def group(g, _):
        transform(
            [2 * g, 2 * g + 1], nt, stations, held[0], held[1], held[2:], xs, obuf
        )
        return 0

    lax.fori_loop(0, stations // 2, group, 0, unroll=2)
    write_messages(nt, 0, stations, obuf, mbuf, msgs, out_sem)


def late_kernel(half, skip, at_row, *refs):
    stream, given, tables, trail = refs[0], refs[1:3], refs[3:7], refs[7]
    final = half == HALVES - 1
    outs = refs[10:] if final else refs[8:]
    if half and not final:
        outs = refs[9:]
    obuf, rest = outs[0], outs[1:]
    if final:
        msgs, mbuf, out_sem = rest[:3]
        rest = rest[3:]
    xin, xs, in_sem, small_sem = rest[:4]
    held = rest[4:]
    stations = stream.shape[0]
    some = trail.shape[0]
    pitch = xs.shape[0] // stations
    copy = pltpu.make_async_copy(stream.at[:, pl.ds(skip, FA * LANES)], xin, in_sem)
    small = [
        pltpu.make_async_copy(source, target, small_sem.at[i])
        for i, (source, target) in enumerate(zip(given, held))
    ]
    for begun in [copy] + small:
        begun.start()
    spread(trail, 0, xs, half * some * pitch + FA, pitch)
    copy.wait()
    spread(xin, 0, xs, 0, pitch)
    xs[pl.ds(FA + ROWS, stations, stride=pitch), :] = jnp.zeros((stations, LANES), f32)
    for copy in small:
        copy.wait()
    chosen = [half * some + k for k in range(some)]
    transform(chosen, 1, stations, held[0], held[1], tables, xs, obuf)
    if final:
        write_messages(1, at_row, stations, obuf, mbuf, msgs, out_sem)


def odd_pitch(rows):
    return (rows // 16 + 1) * 16 + 8


def scalars(delays, valid):
    return [pltpu.SMEM(delays.shape, delays.dtype), pltpu.SMEM(valid.shape, valid.dtype)]


def early_messages(stream, delays, valid, tables):
    stations = stream.shape[0]
    far = pl.BlockSpec(memory_space=pltpu.HBM)
    here = stream.shape[1] // (FA * LANES)
    nt = here - 1
    return pl.pallas_call(
        lambda *refs: early_kernel(nt, *refs),
        out_shape=jax.ShapeDtypeStruct((NQ * NHI, here * stations, LANES), bf16),
        in_specs=[far] * 7,
        out_specs=pl.BlockSpec(memory_space=pl.ANY),
        scratch_shapes=[
            pltpu.VMEM(stream.shape, bf16),
            pltpu.VMEM((stations * odd_pitch(here * FA), LANES), f32),
            pltpu.VMEM((NHI * nt * stations * OPITCH, LANES), f32),
            pltpu.VMEM((NQ * NHI, nt * stations, LANES), bf16),
            pltpu.SemaphoreType.DMA((here,)),
            pltpu.SemaphoreType.DMA((PIECES,)),
            pltpu.SemaphoreType.DMA((2 + len(tables),)),
        ]
        + scalars(delays, valid)
        + [pltpu.VMEM(table.shape, table.dtype) for table in tables],
        compiler_params=pltpu.CompilerParams(vmem_limit_bytes=28 << 20),
        name="channelize",
    )(*[off_chip(value) for value in (stream, delays, valid, *tables)])


def late_messages(half, stream, delays, valid, tables, trail, so_far):
    stations = stream.shape[0]
    far = pl.BlockSpec(memory_space=pltpu.HBM)
    vmem = pl.BlockSpec(memory_space=pltpu.VMEM)
    hbm = pl.BlockSpec(memory_space=pl.ANY)
    chunk = FA * LANES
    here = stream.shape[1] // chunk
    final = half == HALVES - 1
    args = [off_chip(value) for value in (stream, delays, valid)]
    args += [on_chip(value) for value in (*tables, trail)]
    specs = [far] * 3 + [vmem] * 5
    outs = [pltpu.VMEM((NHI * stations * OPITCH, LANES), f32)]
    out_specs = [vmem]
    scratch = []
    aliases = {}
    if half:
        aliases[8] = 0
        args.append(on_chip(so_far[0]))
        specs.append(vmem)
    if final:
        msgs = so_far[1]
        aliases[9] = 1
        args.append(msgs)
        specs.append(hbm)
        outs.append(jax.ShapeDtypeStruct(msgs.shape, bf16))
        out_specs.append(hbm)
        scratch = [
            pltpu.VMEM((NQ * NHI, stations, LANES), bf16),
            pltpu.SemaphoreType.DMA((PIECES,)),
        ]
    return pl.pallas_call(
        lambda *refs: late_kernel(half, (here - 1) * chunk, (here - 1) * stations, *refs),
        out_shape=outs,
        in_specs=specs,
        out_specs=out_specs,
        scratch_shapes=scratch
        + [
            pltpu.VMEM((stations, chunk), bf16),
            pltpu.VMEM((stations * odd_pitch(FA + ROWS), LANES), f32),
            pltpu.SemaphoreType.DMA(()),
            pltpu.SemaphoreType.DMA((2,)),
        ]
        + scalars(delays, valid),
        input_output_aliases=aliases,
        compiler_params=pltpu.CompilerParams(vmem_limit_bytes=20 << 20),
        name="channelize_late",
    )(*args)


def tone_kernel(tones, msgs, picks, sums):
    stations, count = tones.shape
    places, rows, _ = msgs.shape

    def add_times(p, _):
        tile = msgs[p].astype(f32)
        total = tile[:stations]
        for t in range(1, rows // stations):
            total = total + tile[t * stations : (t + 1) * stations]
        sums[pl.ds(pl.multiple_of(p * stations, stations), stations), :] = total
        return 0

    lax.fori_loop(0, places, add_times, 0, unroll=8)
    sub = lax.broadcasted_iota(jnp.int32, (stations, LANES), 0)
    slot = lax.broadcasted_iota(jnp.int32, (stations, LANES), 1) % NTONE

    def one_tone(k, acc):
        here = jnp.where(slot == k, sub, -1)
        for s in range(stations):
            chan = tones[s, k]
            place = lax.shift_right_logical(chan, LO.bit_length() - 1)
            within = lax.bitwise_and(chan, LO - 1)
            total = sums[pl.ds(pl.multiple_of(place * stations, stations), stations), :]
            turned = pltpu.roll(total, lax.bitwise_and(k - within, LANES - 1), 1)
            acc = jnp.where(here == s, turned, acc)
        return acc

    picks[...] = lax.fori_loop(0, count, one_tone, jnp.zeros((stations, LANES), f32), unroll=4)


def tone_sums(msgs, tone_chan):
    return pl.pallas_call(
        tone_kernel,
        out_shape=jax.ShapeDtypeStruct((tone_chan.shape[0], 2 * NTONE), f32),
        in_specs=[
            pl.BlockSpec(memory_space=pltpu.SMEM),
            pl.BlockSpec(memory_space=pltpu.VMEM),
        ],
        out_specs=pl.BlockSpec(memory_space=pltpu.VMEM),
        scratch_shapes=[pltpu.VMEM((msgs.shape[0] * tone_chan.shape[0], LANES), f32)],
        compiler_params=pltpu.CompilerParams(vmem_limit_bytes=8 << 20),
        name="tones",
    )(tone_chan, msgs)


PITCH = 136


def x_kernel(norm_scale, per_source, recv, vis, rs, ts, gs, block, out_sem):
    sources, rows, _ = recv.shape
    local = per_source
    groups = S // local
    times = sources // groups * rows // local

    def widen(i, _):
        at = pl.multiple_of(i * rows, rows)
        rs[pl.ds(at, rows), :] = recv[i].astype(f32)
        return 0

    lax.fori_loop(0, sources, widen, 0, unroll=8)

    def turn(i, _):
        g = i // local
        s = i - g * local
        got = rs[pl.ds(g * times * local + s, times, stride=local), :]
        ts[pl.ds(pl.multiple_of(i * PITCH, 8), LANES), :] = got.T
        return 0

    lax.fori_loop(0, S, turn, 0, unroll=True)

    lane = lax.broadcasted_iota(jnp.int32, (8, LANES), 1)

    sent = []

    def eight(o, _):
        base = o * 8
        for c in range(8):
            re = ts[pl.ds(base + c, S, stride=PITCH), :]
            im = ts[pl.ds(base + c + LO, S, stride=PITCH), :]
            plus, quad, minus = re.astype(bf16), im.astype(bf16), (-re).astype(bf16)
            straight = jnp.concatenate([plus, quad], axis=1)
            turned = jnp.concatenate([quad, minus], axis=1)
            left = jnp.concatenate([straight, turned], axis=0)
            right = jnp.concatenate([straight, straight], axis=0)
            gram = lax.dot_general(
                left, right, (((1,), (1,)), ((), ())), preferred_element_type=f32
            )
            gs[pl.ds(c * PITCH, 2 * S), :] = gram * norm_scale
        top = base
        for j in range(S):
            even = gs[pl.ds(2 * j, 8, stride=PITCH), :]
            odd = gs[pl.ds(2 * j + 1, 8, stride=PITCH), :]
            block[pl.ds(top, 8), pl.ds(j * LANES, LANES)] = jnp.where(lane < S, even, odd)
        return 0

    for o in range(LO // 8):
        eight(o, 0)
        sent.append(
            pltpu.make_async_copy(
                block.at[pl.ds(o * 8, 8), :], vis.at[pl.ds(o * 8, 8), :], out_sem.at[o]
            )
        )
        sent[o].start()
    for copy in sent:
        copy.wait()


def correlated(recv, per_source, norm_scale):
    vmem = pl.BlockSpec(memory_space=pltpu.VMEM)
    return pl.pallas_call(
        lambda *refs: x_kernel(norm_scale, per_source, *refs),
        out_shape=jax.ShapeDtypeStruct((LO, 2 * S * S), f32),
        in_specs=[vmem],
        out_specs=pl.BlockSpec(memory_space=pl.ANY),
        scratch_shapes=[
            pltpu.VMEM((recv.shape[0] * recv.shape[1], LANES), f32),
            pltpu.VMEM((S * PITCH, LANES), f32),
            pltpu.VMEM((8 * PITCH, LANES), f32),
            pltpu.VMEM((LO, 2 * S * S), f32),
            pltpu.SemaphoreType.DMA((LO // 8,)),
        ],
        compiler_params=pltpu.CompilerParams(vmem_limit_bytes=24 << 20),
        name="correlate",
    )(on_chip(recv))


def passed_along(block, axis, distance):
    devices = range(lax.axis_size(axis))
    route = [(i - distance, i) for i in devices if i - distance in devices]
    return lax.ppermute(block, axis, route)


def routed(value, axis, dest):
    return lax.ppermute(value, axis, [(i, dest(i)) for i in range(lax.axis_size(axis))])


def gathered_sum(picks):
    value = picks + routed(picks, "cores", lambda i: i ^ 1)
    value = value + routed(value, "tm", lambda i: i ^ 1)
    size = lax.axis_size("tm")
    half = size // 4
    steps = [
        routed(value, "tm", lambda i, d=d: (i + 2 * (d + half * (i % 2))) % size)
        for d in range(half)
    ]
    value = sum(steps)
    return value + routed(value, "tm", lambda i: i ^ 1)


def shards(samples, delays, valid, tone_chan):
    stations, stretch = samples.shape
    whole = ("stn", "tm", "cores")
    here = stretch // (FA * FB)
    some = stations // HALVES
    trailing = [
        passed_along(samples[i * some : (i + 1) * some, :MAXD], ("tm", "cores"), -1)
        for i in range(HALVES)
    ]
    tables = [jnp.asarray(table) for table in make_tables()]
    own = (samples, delays, valid, tables)
    early = early_messages(*own)
    (held,) = late_messages(0, *own, trailing[0], ())
    _, msgs = late_messages(1, *own, trailing[1], (held, early))
    spectra_all = here * lax.axis_size("tm") * lax.axis_size("cores")
    norm_scale = 1.0 / math.sqrt(spectra_all)
    recv = lax.all_to_all(msgs, whole, split_axis=0, concat_axis=0, tiled=True)
    phase_cal = gathered_sum(tone_sums(msgs, tone_chan)) * norm_scale
    return (correlated(recv, stations, norm_scale), phase_cal)


def solution(mesh):
    return jax.shard_map(
        shards,
        mesh=mesh,
        in_specs=(P("stn", ("tm", "cores")), P("stn"), P("stn"), P("stn", None)),
        out_specs=(P(("stn", "tm", "cores"), None), P("stn", None)),
        check_vma=False,
    )
```

```python
import math

import jax
import jax.numpy as jnp
import ml_dtypes
import numpy as np
from jax import lax
from jax.experimental import pallas as pl
from jax.experimental.pallas import tpu as pltpu
from jax.sharding import PartitionSpec as P

S = 64
NCH = 16384
FA = 256
FB = 128
NTONE = 64
MAXD = 32768
NQ = FB // 2
NHI = 4
LO = FA // NHI
LANES = 128

f32 = jnp.float32
bf16 = jnp.bfloat16


def make_tables():
    k1 = np.arange(FA)
    angles = 2.0 * np.pi / FA * (k1[:, None] * k1[None, :] % FA)
    section_one = np.concatenate([np.cos(angles), -np.sin(angles)], axis=1).astype(
        ml_dtypes.bfloat16
    )
    n2 = np.arange(FB)
    length = FA * FB
    twists = 2.0 * np.pi / length * (n2[:, None] * k1[None, :] % length)
    scale = 1.0 / math.sqrt(length)
    twist_cos = (np.cos(twists) * scale).astype(np.float32)
    twist_sin = (np.sin(twists) * scale).astype(np.float32)
    q = np.arange(NQ)
    thetas = 2.0 * np.pi / FB * (q[:, None] * n2[None, :] % FB)
    cosine, sine = np.cos(thetas), np.sin(thetas)
    section_two = np.block([[cosine, sine], [-sine, cosine]]).astype(ml_dtypes.bfloat16)
    return (section_one, twist_cos, twist_sin, section_two)


OPITCH = NQ + 8
PIECES = 4
GROUP = (8, 2)
UNROLL = (1, 2)


def f_kernel(nt, skip, at_row, more, *refs):
    stream, refs, given = refs[0], refs[7:], refs[1:7]
    trail = refs[0] if more else None
    msgs = refs[2 if more else 0]
    xin, xs, obuf, mbuf, in_sem, out_sem, small_sem = refs[-13:-6]
    held = refs[-6:]
    if more:
        given, held, tables = given[:2], held[:2], given[2:]
    else:
        tables = held[2:]
    delays, valid = held[:2]
    one, tcos, tsin, two = tables
    small = [
        pltpu.make_async_copy(source, target, small_sem.at[i])
        for i, (source, target) in enumerate(zip(given, held))
    ]
    stations = stream.shape[0]
    rows = nt * FA
    chunk = FA * LANES
    pitch = xs.shape[0] // stations
    copies = [
        pltpu.make_async_copy(
            stream.at[:, pl.ds(skip + i * chunk, chunk)],
            xin.at[:, pl.ds(i * chunk, chunk)],
            in_sem.at[i],
        )
        for i in range(xin.shape[1] // chunk)
    ]
    for copy in copies + small:
        copy.start()

    def spread(source, base, to):
        def one_row(j, _):
            at = pl.multiple_of((base + j) * LANES, LANES)
            xs[pl.ds(to + j, stations, stride=pitch), :] = source[:, pl.ds(at, LANES)].astype(
                f32
            )
            return 0

        lax.fori_loop(0, FA, one_row, 0, unroll=16)

    filled = len(copies) * FA
    if more:
        spread(trail, 0, filled)
    for i, copy in enumerate(copies):
        copy.wait()
        spread(xin, i * FA, i * FA)
    if more:
        filled += FA
    xs[pl.ds(filled, stations, stride=pitch), :] = jnp.zeros((stations, LANES), f32)
    for copy in small:
        copy.wait()
    src = lax.broadcasted_iota(jnp.int32, (2 * LANES, LANES), 0)
    dst = lax.broadcasted_iota(jnp.int32, (2 * LANES, LANES), 1)
    low = lax.broadcasted_iota(jnp.int32, (NQ, LANES), 1) < LO

    def group(g, _):
        blocks = []
        for k in range(GROUP[nt > 1]):
            s = g * GROUP[nt > 1] + k
            shift = delays[s]
            lead = shift // LANES
            within = shift - lead * LANES
            first = xs[pl.ds(s * pitch + lead, rows), :]
            second = xs[pl.ds(s * pitch + lead + 1, rows), :]
            pair = jnp.concatenate([first.astype(bf16), second.astype(bf16)], axis=1)
            move = (src == dst + within).astype(f32).astype(bf16)
            moved = jnp.dot(pair, move, preferred_element_type=f32).astype(bf16)
            blocks += [moved[t * FA : (t + 1) * FA] for t in range(nt)]
        sections = lax.dot_general(
            jnp.concatenate(blocks, axis=1),
            one[...],
            (((0,), (0,)), ((), ())),
            preferred_element_type=f32,
        )
        for k in range(GROUP[nt > 1]):
            s = g * GROUP[nt > 1] + k
            last = (two[...].astype(f32) * valid[s].astype(f32)).astype(bf16)
            for t in range(nt):
                at = (k * nt + t) * FB
                re, im = sections[at : at + FB, :FA], sections[at : at + FB, FA:]
                cosine, sine = tcos[...], tsin[...]
                tr = (re * cosine + im * sine).astype(bf16)
                ti = (im * cosine - re * sine).astype(bf16)
                spec = jnp.dot(
                    last, jnp.concatenate([tr, ti], axis=0), preferred_element_type=f32
                )
                for j in range(FA // LANES):
                    a = spec[:NQ, j * LANES : (j + 1) * LANES]
                    b = spec[NQ:, j * LANES : (j + 1) * LANES]
                    even = jnp.where(low, a, pltpu.roll(b, LO, 1))
                    odd = jnp.where(low, pltpu.roll(a, LO, 1), b)
                    for h, piece in ((2 * j, even), (2 * j + 1, odd)):
                        to = pl.multiple_of(((h * nt + t) * stations + s) * OPITCH, 8)
                        obuf[pl.ds(to, NQ), :] = piece
        return 0

    lax.fori_loop(0, stations // GROUP[nt > 1], group, 0, unroll=UNROLL[nt > 1])

    per = NQ // PIECES
    sent = []
    for i in range(PIECES):

        def gather(q, _):
            for h in range(NHI):
                got = obuf[
                    pl.ds(h * nt * stations * OPITCH + q, nt * stations, stride=OPITCH), :
                ]
                mbuf[q * NHI + h] = got.astype(bf16)
            return 0

        lax.fori_loop(i * per, (i + 1) * per, gather, 0, unroll=4)
        span = pl.ds(i * per * NHI, per * NHI)
        sent.append(
            pltpu.make_async_copy(
                mbuf.at[span], msgs.at[span, pl.ds(at_row, nt * stations), :], out_sem.at[i]
            )
        )
        sent[i].start()
    for copy in sent:
        copy.wait()


def on_chip(value):
    return pltpu.with_memory_space_constraint(value, pltpu.VMEM)


def off_chip(value):
    return pltpu.with_memory_space_constraint(value, pltpu.HBM)


def channelized(stream, delays, valid, tables, so_far=()):
    stations = stream.shape[0]
    hbm = pl.BlockSpec(memory_space=pl.ANY)
    vmem = pl.BlockSpec(memory_space=pltpu.VMEM)
    chunk = FA * LANES
    here = stream.shape[1] // chunk
    far = pl.BlockSpec(memory_space=pltpu.HBM)
    tables = [jnp.asarray(table) for table in tables]
    if so_far:
        msgs, trailing = so_far
        nt, skip, at_row = 1, (here - 1) * chunk, (here - 1) * stations
        extra = (on_chip(trailing), msgs)
        specs = [far] * 3 + [vmem] * 5 + [hbm]
        tables = [on_chip(table) for table in tables]
        aliases = {8: 0}
        held = 1
    else:
        nt, skip, at_row, extra = here - 1, 0, 0, ()
        aliases = {}
        held = here
        specs = [far] * 7
        tables = [off_chip(table) for table in tables]
    pitch = ((held + len(aliases)) * FA // 16 + 1) * 16 + 8
    return pl.pallas_call(
        lambda *refs: f_kernel(nt, skip, at_row, bool(so_far), *refs),
        out_shape=jax.ShapeDtypeStruct((NQ * NHI, here * stations, LANES), bf16),
        in_specs=specs,
        out_specs=hbm,
        scratch_shapes=[
            pltpu.VMEM((stations, held * chunk), bf16),
            pltpu.VMEM((stations * pitch, LANES), f32),
            pltpu.VMEM((NHI * nt * stations * OPITCH, LANES), f32),
            pltpu.VMEM((NQ * NHI, nt * stations, LANES), bf16),
            pltpu.SemaphoreType.DMA((held,)),
            pltpu.SemaphoreType.DMA((PIECES,)),
            pltpu.SemaphoreType.DMA((2 + len(tables),)),
            pltpu.SMEM(delays.shape, delays.dtype),
            pltpu.SMEM(valid.shape, valid.dtype),
        ]
        + [pltpu.VMEM(table.shape, table.dtype) for table in tables],
        input_output_aliases=aliases,
        compiler_params=pltpu.CompilerParams(vmem_limit_bytes=28 << 20),
        name="channelize",
    )(*[off_chip(value) for value in (stream, delays, valid)], *tables, *extra)


def tone_kernel(tones, msgs, picks, sums):
    stations, count = tones.shape
    places, rows, _ = msgs.shape

    def add_times(p, _):
        tile = msgs[p].astype(f32)
        total = tile[:stations]
        for t in range(1, rows // stations):
            total = total + tile[t * stations : (t + 1) * stations]
        sums[pl.ds(pl.multiple_of(p * stations, stations), stations), :] = total
        return 0

    lax.fori_loop(0, places, add_times, 0, unroll=8)
    sub = lax.broadcasted_iota(jnp.int32, (stations, LANES), 0)
    slot = lax.broadcasted_iota(jnp.int32, (stations, LANES), 1) % NTONE

    def one_tone(k, acc):
        here = jnp.where(slot == k, sub, -1)
        for s in range(stations):
            chan = tones[s, k]
            place = lax.shift_right_logical(chan, LO.bit_length() - 1)
            within = lax.bitwise_and(chan, LO - 1)
            total = sums[pl.ds(pl.multiple_of(place * stations, stations), stations), :]
            turned = pltpu.roll(total, lax.bitwise_and(k - within, LANES - 1), 1)
            acc = jnp.where(here == s, turned, acc)
        return acc

    picks[...] = lax.fori_loop(0, count, one_tone, jnp.zeros((stations, LANES), f32), unroll=4)


def tone_sums(msgs, tone_chan):
    return pl.pallas_call(
        tone_kernel,
        out_shape=jax.ShapeDtypeStruct((tone_chan.shape[0], 2 * NTONE), f32),
        in_specs=[
            pl.BlockSpec(memory_space=pltpu.SMEM),
            pl.BlockSpec(memory_space=pltpu.VMEM),
        ],
        out_specs=pl.BlockSpec(memory_space=pltpu.VMEM),
        scratch_shapes=[pltpu.VMEM((msgs.shape[0] * tone_chan.shape[0], LANES), f32)],
        compiler_params=pltpu.CompilerParams(vmem_limit_bytes=8 << 20),
        name="tones",
    )(tone_chan, msgs)


PITCH = 136


def x_kernel(norm_scale, per_source, recv, vis, rs, ts, gs, block, out_sem):
    sources, rows, _ = recv.shape
    local = per_source
    groups = S // local
    times = sources // groups * rows // local

    def widen(i, _):
        at = pl.multiple_of(i * rows, rows)
        rs[pl.ds(at, rows), :] = recv[i].astype(f32)
        return 0

    lax.fori_loop(0, sources, widen, 0, unroll=8)

    def turn(i, _):
        g = i // local
        s = i - g * local
        got = rs[pl.ds(g * times * local + s, times, stride=local), :]
        ts[pl.ds(pl.multiple_of(i * PITCH, 8), LANES), :] = got.astype(bf16).T.astype(f32)
        return 0

    lax.fori_loop(0, S, turn, 0, unroll=True)

    lane = lax.broadcasted_iota(jnp.int32, (8, LANES), 1)

    sent = []

    def eight(o, _):
        base = o * 8
        for c in range(8):
            re = ts[pl.ds(base + c, S, stride=PITCH), :]
            im = ts[pl.ds(base + c + LO, S, stride=PITCH), :]
            plus, quad, minus = re.astype(bf16), im.astype(bf16), (-re).astype(bf16)
            straight = jnp.concatenate([plus, quad], axis=1)
            turned = jnp.concatenate([quad, minus], axis=1)
            left = jnp.concatenate([straight, turned], axis=0)
            right = jnp.concatenate([straight, straight], axis=0)
            gram = lax.dot_general(
                left, right, (((1,), (1,)), ((), ())), preferred_element_type=f32
            )
            gs[pl.ds(c * PITCH, 2 * S), :] = gram * norm_scale
        top = base
        for j in range(S):
            even = gs[pl.ds(2 * j, 8, stride=PITCH), :]
            odd = gs[pl.ds(2 * j + 1, 8, stride=PITCH), :]
            block[pl.ds(top, 8), pl.ds(j * LANES, LANES)] = jnp.where(lane < S, even, odd)
        return 0

    for o in range(LO // 8):
        eight(o, 0)
        sent.append(
            pltpu.make_async_copy(
                block.at[pl.ds(o * 8, 8), :], vis.at[pl.ds(o * 8, 8), :], out_sem.at[o]
            )
        )
        sent[o].start()
    for copy in sent:
        copy.wait()


def correlated(recv, per_source, norm_scale):
    vmem = pl.BlockSpec(memory_space=pltpu.VMEM)
    return pl.pallas_call(
        lambda *refs: x_kernel(norm_scale, per_source, *refs),
        out_shape=jax.ShapeDtypeStruct((LO, 2 * S * S), f32),
        in_specs=[vmem],
        out_specs=pl.BlockSpec(memory_space=pl.ANY),
        scratch_shapes=[
            pltpu.VMEM((recv.shape[0] * recv.shape[1], LANES), f32),
            pltpu.VMEM((S * PITCH, LANES), f32),
            pltpu.VMEM((8 * PITCH, LANES), f32),
            pltpu.VMEM((LO, 2 * S * S), f32),
            pltpu.SemaphoreType.DMA((LO // 8,)),
        ],
        compiler_params=pltpu.CompilerParams(vmem_limit_bytes=24 << 20),
        name="correlate",
    )(on_chip(recv))


def passed_along(block, axis, distance):
    devices = range(lax.axis_size(axis))
    route = [(i - distance, i) for i in devices if i - distance in devices]
    return lax.ppermute(block, axis, route)


def routed(value, axis, dest):
    return lax.ppermute(value, axis, [(i, dest(i)) for i in range(lax.axis_size(axis))])


def over_z(picks):
    value = picks + routed(picks, "cores", lambda i: i ^ 1)
    value = value + routed(value, "tm", lambda i: i ^ 1)
    size = lax.axis_size("tm")
    half = size // 4
    steps = [
        routed(value, "tm", lambda i, d=d: (i + 2 * (d + half * (i % 2))) % size)
        for d in range(half)
    ]
    return sum(steps)


def shards(samples, delays, valid, tone_chan):
    stations, stretch = samples.shape
    whole = ("stn", "tm", "cores")
    here = stretch // (FA * FB)
    trailing = passed_along(samples[:, :MAXD], ("tm", "cores"), -1)
    own = (samples, delays, valid, make_tables())
    msgs = channelized(*own, (channelized(*own), trailing))
    spectra_all = here * lax.axis_size("tm") * lax.axis_size("cores")
    norm_scale = 1.0 / math.sqrt(spectra_all)
    recv = lax.all_to_all(msgs, whole, split_axis=0, concat_axis=0, tiled=True)
    half = over_z(tone_sums(msgs, tone_chan)) * norm_scale
    recv, half = lax.optimization_barrier((recv, half))
    phase_cal = half + routed(half, "tm", lambda i: i ^ 1)
    return (correlated(recv, stations, norm_scale), phase_cal)


def solution(mesh):
    return jax.shard_map(
        shards,
        mesh=mesh,
        in_specs=(P("stn", ("tm", "cores")), P("stn"), P("stn"), P("stn", None)),
        out_specs=(P(("stn", "tm", "cores"), None), P("stn", None)),
        check_vma=False,
    )
```

```python
import math

import jax
import jax.numpy as jnp
import ml_dtypes
import numpy as np
from jax import lax
from jax.experimental import pallas as pl
from jax.experimental.pallas import tpu as pltpu
from jax.sharding import PartitionSpec as P

S = 64
NCH = 16384
FA = 256
FB = 128
NTONE = 64
MAXD = 32768
NQ = FB // 2
NHI = 4
LO = FA // NHI
LANES = 128

f32 = jnp.float32
bf16 = jnp.bfloat16


def make_tables():
    k1 = np.arange(FA)
    angles = 2.0 * np.pi / FA * (k1[:, None] * k1[None, :] % FA)
    section_one = np.concatenate([np.cos(angles), -np.sin(angles)], axis=1).astype(
        ml_dtypes.bfloat16
    )
    n2 = np.arange(FB)
    length = FA * FB
    twists = 2.0 * np.pi / length * (n2[:, None] * k1[None, :] % length)
    scale = 1.0 / math.sqrt(length)
    twist_cos = (np.cos(twists) * scale).astype(np.float32)
    twist_sin = (np.sin(twists) * scale).astype(np.float32)
    q = np.arange(NQ)
    thetas = 2.0 * np.pi / FB * (q[:, None] * n2[None, :] % FB)
    cosine, sine = np.cos(thetas), np.sin(thetas)
    section_two = np.block([[cosine, sine], [-sine, cosine]]).astype(ml_dtypes.bfloat16)
    return (section_one, twist_cos, twist_sin, section_two)


OPITCH = NQ + 8
PIECES = 4
ROWS = MAXD // LANES


def on_chip(value):
    return pltpu.with_memory_space_constraint(value, pltpu.VMEM)


def off_chip(value):
    return pltpu.with_memory_space_constraint(value, pltpu.HBM)


def spread(source, base, xs, first, stride):
    def one_row(j, _):
        at = pl.multiple_of((base + j) * LANES, LANES)
        xs[pl.ds(first + j, source.shape[0], stride=stride), :] = source[
            :, pl.ds(at, LANES)
        ].astype(f32)
        return 0

    lax.fori_loop(0, FA, one_row, 0, unroll=16)


def transform(chosen, nt, stations, delays, valid, tables, xs, obuf):
    one, tcos, tsin, two = tables
    rows = nt * FA
    pitch = xs.shape[0] // stations
    src = lax.broadcasted_iota(jnp.int32, (2 * LANES, LANES), 0)
    dst = lax.broadcasted_iota(jnp.int32, (2 * LANES, LANES), 1)
    low = lax.broadcasted_iota(jnp.int32, (NQ, LANES), 1) < LO
    blocks = []
    for s in chosen:
        shift = delays[s]
        lead = shift // LANES
        within = shift - lead * LANES
        first = xs[pl.ds(s * pitch + lead, rows), :]
        second = xs[pl.ds(s * pitch + lead + 1, rows), :]
        pair = jnp.concatenate([first.astype(bf16), second.astype(bf16)], axis=1)
        move = (src == dst + within).astype(f32).astype(bf16)
        moved = jnp.dot(pair, move, preferred_element_type=f32).astype(bf16)
        blocks += [moved[t * FA : (t + 1) * FA] for t in range(nt)]
    sections = lax.dot_general(
        jnp.concatenate(blocks, axis=1),
        one[...],
        (((0,), (0,)), ((), ())),
        preferred_element_type=f32,
    )
    for k, s in enumerate(chosen):
        last = (two[...].astype(f32) * valid[s].astype(f32)).astype(bf16)
        for t in range(nt):
            at = (k * nt + t) * FB
            re, im = sections[at : at + FB, :FA], sections[at : at + FB, FA:]
            cosine, sine = tcos[...], tsin[...]
            tr = (re * cosine + im * sine).astype(bf16)
            ti = (im * cosine - re * sine).astype(bf16)
            spec = jnp.dot(last, jnp.concatenate([tr, ti], axis=0), preferred_element_type=f32)
            for j in range(FA // LANES):
                a = spec[:NQ, j * LANES : (j + 1) * LANES]
                b = spec[NQ:, j * LANES : (j + 1) * LANES]
                even = jnp.where(low, a, pltpu.roll(b, LO, 1))
                odd = jnp.where(low, pltpu.roll(a, LO, 1), b)
                for h, piece in ((2 * j, even), (2 * j + 1, odd)):
                    to = ((h * nt + t) * stations + s) * OPITCH
                    obuf[pl.ds(pl.multiple_of(to, 8), NQ), :] = piece


def write_messages(nt, at_row, stations, obuf, mbuf, msgs, out_sem):
    per = NQ // PIECES
    sent = []
    for i in range(PIECES):

        def gather(q, _):
            for h in range(NHI):
                got = obuf[
                    pl.ds(h * nt * stations * OPITCH + q, nt * stations, stride=OPITCH), :
                ]
                mbuf[q * NHI + h] = got.astype(bf16)
            return 0

        lax.fori_loop(i * per, (i + 1) * per, gather, 0, unroll=4)
        span = pl.ds(i * per * NHI, per * NHI)
        sent.append(
            pltpu.make_async_copy(
                mbuf.at[span], msgs.at[span, pl.ds(at_row, nt * stations), :], out_sem.at[i]
            )
        )
        sent[i].start()
    for copy in sent:
        copy.wait()


def early_kernel(nt, *refs):
    stream, given, msgs, handed = refs[0], refs[1:7], refs[7], refs[8]
    xin, xs, obuf, mbuf, in_sem, out_sem, small_sem = refs[9:16]
    held = refs[16:]
    stations = stream.shape[0]
    chunk = FA * LANES
    pitch = xs.shape[0] // stations
    copies = [
        pltpu.make_async_copy(
            stream.at[:, pl.ds(i * chunk, chunk)],
            xin.at[:, pl.ds(i * chunk, chunk)],
            in_sem.at[i],
        )
        for i in range(nt + 1)
    ]
    small = [
        pltpu.make_async_copy(source, target, small_sem.at[i])
        for i, (source, target) in enumerate(zip(given, held))
    ]
    for copy in copies + small:
        copy.start()
    for i, copy in enumerate(copies):
        copy.wait()
        spread(xin, i * FA, xs, i * FA, pitch)
    spread(xin, nt * FA, handed, 0, handed.shape[0] // stations)
    xs[pl.ds((nt + 1) * FA, stations, stride=pitch), :] = jnp.zeros((stations, LANES), f32)
    for copy in small:
        copy.wait()

    def group(g, _):
        transform(
            [2 * g, 2 * g + 1], nt, stations, held[0], held[1], held[2:], xs, obuf
        )
        return 0

    lax.fori_loop(0, stations // 2, group, 0, unroll=2)
    write_messages(nt, 0, stations, obuf, mbuf, msgs, out_sem)


def late_kernel(at_row, *refs):
    given, tables, trail = refs[:2], refs[2:6], refs[6]
    xs, msgs, obuf, mbuf, out_sem, small_sem = refs[9:15]
    held = refs[15:]
    stations = trail.shape[0]
    pitch = xs.shape[0] // stations
    small = [
        pltpu.make_async_copy(source, target, small_sem.at[i])
        for i, (source, target) in enumerate(zip(given, held))
    ]
    for copy in small:
        copy.start()
    spread(trail, 0, xs, FA, pitch)
    xs[pl.ds(FA + ROWS, stations, stride=pitch), :] = jnp.zeros((stations, LANES), f32)
    for copy in small:
        copy.wait()
    transform(range(stations), 1, stations, held[0], held[1], tables, xs, obuf)
    write_messages(1, at_row, stations, obuf, mbuf, msgs, out_sem)


def odd_pitch(rows):
    return (rows // 16 + 1) * 16 + 8


def scalars(delays, valid):
    return [pltpu.SMEM(delays.shape, delays.dtype), pltpu.SMEM(valid.shape, valid.dtype)]


def early_messages(stream, delays, valid, tables):
    stations = stream.shape[0]
    far = pl.BlockSpec(memory_space=pltpu.HBM)
    here = stream.shape[1] // (FA * LANES)
    nt = here - 1
    return pl.pallas_call(
        lambda *refs: early_kernel(nt, *refs),
        out_shape=(
            jax.ShapeDtypeStruct((NQ * NHI, here * stations, LANES), bf16),
            pltpu.VMEM((stations * odd_pitch(FA + ROWS), LANES), f32),
        ),
        in_specs=[far] * 7,
        out_specs=(pl.BlockSpec(memory_space=pl.ANY), pl.BlockSpec(memory_space=pltpu.VMEM)),
        scratch_shapes=[
            pltpu.VMEM(stream.shape, bf16),
            pltpu.VMEM((stations * odd_pitch(here * FA), LANES), f32),
            pltpu.VMEM((NHI * nt * stations * OPITCH, LANES), f32),
            pltpu.VMEM((NQ * NHI, nt * stations, LANES), bf16),
            pltpu.SemaphoreType.DMA((here,)),
            pltpu.SemaphoreType.DMA((PIECES,)),
            pltpu.SemaphoreType.DMA((2 + len(tables),)),
        ]
        + scalars(delays, valid)
        + [pltpu.VMEM(table.shape, table.dtype) for table in tables],
        compiler_params=pltpu.CompilerParams(vmem_limit_bytes=28 << 20),
        name="channelize",
    )(*[off_chip(value) for value in (stream, delays, valid, *tables)])


def late_messages(delays, valid, tables, trail, msgs, handed):
    stations = trail.shape[0]
    far = pl.BlockSpec(memory_space=pltpu.HBM)
    vmem = pl.BlockSpec(memory_space=pltpu.VMEM)
    hbm = pl.BlockSpec(memory_space=pl.ANY)
    at_row = msgs.shape[1] - stations
    args = [off_chip(value) for value in (delays, valid)]
    args += [on_chip(value) for value in (*tables, trail, handed)]
    return pl.pallas_call(
        lambda *refs: late_kernel(at_row, *refs),
        out_shape=(
            pltpu.VMEM(handed.shape, f32),
            jax.ShapeDtypeStruct(msgs.shape, bf16),
        ),
        in_specs=[far] * 2 + [vmem] * 6 + [hbm],
        out_specs=(vmem, hbm),
        scratch_shapes=[
            pltpu.VMEM((NHI * stations * OPITCH, LANES), f32),
            pltpu.VMEM((NQ * NHI, stations, LANES), bf16),
            pltpu.SemaphoreType.DMA((PIECES,)),
            pltpu.SemaphoreType.DMA((2,)),
        ]
        + scalars(delays, valid),
        input_output_aliases={7: 0, 8: 1},
        compiler_params=pltpu.CompilerParams(vmem_limit_bytes=20 << 20),
        name="channelize_late",
    )(*args, msgs)


def tone_kernel(tones, msgs, picks, sums):
    stations, count = tones.shape
    places, rows, _ = msgs.shape

    def add_times(p, _):
        tile = msgs[p].astype(f32)
        total = tile[:stations]
        for t in range(1, rows // stations):
            total = total + tile[t * stations : (t + 1) * stations]
        sums[pl.ds(pl.multiple_of(p * stations, stations), stations), :] = total
        return 0

    lax.fori_loop(0, places, add_times, 0, unroll=8)
    sub = lax.broadcasted_iota(jnp.int32, (stations, LANES), 0)
    slot = lax.broadcasted_iota(jnp.int32, (stations, LANES), 1) % NTONE

    def one_tone(k, acc):
        here = jnp.where(slot == k, sub, -1)
        for s in range(stations):
            chan = tones[s, k]
            place = lax.shift_right_logical(chan, LO.bit_length() - 1)
            within = lax.bitwise_and(chan, LO - 1)
            total = sums[pl.ds(pl.multiple_of(place * stations, stations), stations), :]
            turned = pltpu.roll(total, lax.bitwise_and(k - within, LANES - 1), 1)
            acc = jnp.where(here == s, turned, acc)
        return acc

    picks[...] = lax.fori_loop(0, count, one_tone, jnp.zeros((stations, LANES), f32), unroll=4)


def tone_sums(msgs, tone_chan):
    return pl.pallas_call(
        tone_kernel,
        out_shape=jax.ShapeDtypeStruct((tone_chan.shape[0], 2 * NTONE), f32),
        in_specs=[
            pl.BlockSpec(memory_space=pltpu.SMEM),
            pl.BlockSpec(memory_space=pltpu.VMEM),
        ],
        out_specs=pl.BlockSpec(memory_space=pltpu.VMEM),
        scratch_shapes=[pltpu.VMEM((msgs.shape[0] * tone_chan.shape[0], LANES), f32)],
        compiler_params=pltpu.CompilerParams(vmem_limit_bytes=8 << 20),
        name="tones",
    )(tone_chan, msgs)


PITCH = 136


def x_kernel(norm_scale, per_source, recv, vis, rs, ts, gs, block, out_sem):
    sources, rows, _ = recv.shape
    local = per_source
    groups = S // local
    times = sources // groups * rows // local

    def widen(i, _):
        at = pl.multiple_of(i * rows, rows)
        rs[pl.ds(at, rows), :] = recv[i].astype(f32)
        return 0

    lax.fori_loop(0, sources, widen, 0, unroll=8)

    def turn(i, _):
        g = i // local
        s = i - g * local
        got = rs[pl.ds(g * times * local + s, times, stride=local), :]
        ts[pl.ds(pl.multiple_of(i * PITCH, 8), LANES), :] = got.astype(bf16).T.astype(f32)
        return 0

    lax.fori_loop(0, S, turn, 0, unroll=True)

    lane = lax.broadcasted_iota(jnp.int32, (8, LANES), 1)

    sent = []

    def eight(o, _):
        base = o * 8
        for c in range(8):
            re = ts[pl.ds(base + c, S, stride=PITCH), :]
            im = ts[pl.ds(base + c + LO, S, stride=PITCH), :]
            plus, quad, minus = re.astype(bf16), im.astype(bf16), (-re).astype(bf16)
            straight = jnp.concatenate([plus, quad], axis=1)
            turned = jnp.concatenate([quad, minus], axis=1)
            left = jnp.concatenate([straight, turned], axis=0)
            right = jnp.concatenate([straight, straight], axis=0)
            gram = lax.dot_general(
                left, right, (((1,), (1,)), ((), ())), preferred_element_type=f32
            )
            gs[pl.ds(c * PITCH, 2 * S), :] = gram * norm_scale
        top = base
        for j in range(S):
            even = gs[pl.ds(2 * j, 8, stride=PITCH), :]
            odd = gs[pl.ds(2 * j + 1, 8, stride=PITCH), :]
            block[pl.ds(top, 8), pl.ds(j * LANES, LANES)] = jnp.where(lane < S, even, odd)
        return 0

    for o in range(LO // 8):
        eight(o, 0)
        sent.append(
            pltpu.make_async_copy(
                block.at[pl.ds(o * 8, 8), :], vis.at[pl.ds(o * 8, 8), :], out_sem.at[o]
            )
        )
        sent[o].start()
    for copy in sent:
        copy.wait()


def correlated(recv, per_source, norm_scale):
    vmem = pl.BlockSpec(memory_space=pltpu.VMEM)
    return pl.pallas_call(
        lambda *refs: x_kernel(norm_scale, per_source, *refs),
        out_shape=jax.ShapeDtypeStruct((LO, 2 * S * S), f32),
        in_specs=[vmem],
        out_specs=pl.BlockSpec(memory_space=pl.ANY),
        scratch_shapes=[
            pltpu.VMEM((recv.shape[0] * recv.shape[1], LANES), f32),
            pltpu.VMEM((S * PITCH, LANES), f32),
            pltpu.VMEM((8 * PITCH, LANES), f32),
            pltpu.VMEM((LO, 2 * S * S), f32),
            pltpu.SemaphoreType.DMA((LO // 8,)),
        ],
        compiler_params=pltpu.CompilerParams(vmem_limit_bytes=24 << 20),
        name="correlate",
    )(on_chip(recv))


def passed_along(block, axis, distance):
    devices = range(lax.axis_size(axis))
    route = [(i - distance, i) for i in devices if i - distance in devices]
    return lax.ppermute(block, axis, route)


def routed(value, axis, dest):
    return lax.ppermute(value, axis, [(i, dest(i)) for i in range(lax.axis_size(axis))])


def gathered_sum(picks):
    value = picks + routed(picks, "cores", lambda i: i ^ 1)
    value = value + routed(value, "tm", lambda i: i ^ 1)
    size = lax.axis_size("tm")
    half = size // 4
    steps = [
        routed(value, "tm", lambda i, d=d: (i + 2 * (d + half * (i % 2))) % size)
        for d in range(half)
    ]
    value = sum(steps)
    return value + routed(value, "tm", lambda i: i ^ 1)


def shards(samples, delays, valid, tone_chan):
    stations, stretch = samples.shape
    whole = ("stn", "tm", "cores")
    here = stretch // (FA * FB)
    trailing = passed_along(samples[:, :MAXD], ("tm", "cores"), -1)
    tables = [jnp.asarray(table) for table in make_tables()]
    early = early_messages(samples, delays, valid, tables)
    _, msgs = late_messages(delays, valid, tables, trailing, *early)
    spectra_all = here * lax.axis_size("tm") * lax.axis_size("cores")
    norm_scale = 1.0 / math.sqrt(spectra_all)
    recv = lax.all_to_all(msgs, whole, split_axis=0, concat_axis=0, tiled=True)
    phase_cal = gathered_sum(tone_sums(msgs, tone_chan)) * norm_scale
    return (correlated(recv, stations, norm_scale), phase_cal)


def solution(mesh):
    return jax.shard_map(
        shards,
        mesh=mesh,
        in_specs=(P("stn", ("tm", "cores")), P("stn"), P("stn"), P("stn", None)),
        out_specs=(P(("stn", "tm", "cores"), None), P("stn", None)),
        check_vma=False,
    )
```

```python
import math

import jax
import jax.numpy as jnp
import ml_dtypes
import numpy as np
from jax import lax
from jax.experimental import pallas as pl
from jax.experimental.pallas import tpu as pltpu
from jax.sharding import PartitionSpec as P

S = 64
NCH = 16384
FA = 256
FB = 128
NTONE = 64
MAXD = 32768
NQ = FB // 2
NHI = 4
LO = FA // NHI
LANES = 128

f32 = jnp.float32
bf16 = jnp.bfloat16


def make_tables():
    k1 = np.arange(FA)
    angles = 2.0 * np.pi / FA * (k1[:, None] * k1[None, :] % FA)
    section_one = np.concatenate([np.cos(angles), -np.sin(angles)], axis=1).astype(
        ml_dtypes.bfloat16
    )
    n2 = np.arange(FB)
    length = FA * FB
    twists = 2.0 * np.pi / length * (n2[:, None] * k1[None, :] % length)
    scale = 1.0 / math.sqrt(length)
    twist_cos = (np.cos(twists) * scale).astype(np.float32)
    twist_sin = (np.sin(twists) * scale).astype(np.float32)
    q = np.arange(NQ)
    thetas = 2.0 * np.pi / FB * (q[:, None] * n2[None, :] % FB)
    cosine, sine = np.cos(thetas), np.sin(thetas)
    section_two = np.block([[cosine, sine], [-sine, cosine]]).astype(ml_dtypes.bfloat16)
    return (section_one, twist_cos, twist_sin, section_two)


OPITCH = NQ + 8
PIECES = 4
ROWS = MAXD // LANES


def on_chip(value):
    return pltpu.with_memory_space_constraint(value, pltpu.VMEM)


def off_chip(value):
    return pltpu.with_memory_space_constraint(value, pltpu.HBM)


def spread(source, base, xs, first, stride):
    def one_row(j, _):
        at = pl.multiple_of((base + j) * LANES, LANES)
        xs[pl.ds(first + j, source.shape[0], stride=stride), :] = source[
            :, pl.ds(at, LANES)
        ].astype(f32)
        return 0

    lax.fori_loop(0, FA, one_row, 0, unroll=32)


def transform(chosen, nt, stations, delays, valid, tables, xs, obuf):
    one, tcos, tsin, two = tables
    rows = nt * FA
    pitch = xs.shape[0] // stations
    src = lax.broadcasted_iota(jnp.int32, (2 * LANES, LANES), 0)
    dst = lax.broadcasted_iota(jnp.int32, (2 * LANES, LANES), 1)
    low = lax.broadcasted_iota(jnp.int32, (NQ, LANES), 1) < LO
    blocks = []
    for s in chosen:
        shift = delays[s]
        lead = shift // LANES
        within = shift - lead * LANES
        first = xs[pl.ds(s * pitch + lead, rows), :]
        second = xs[pl.ds(s * pitch + lead + 1, rows), :]
        pair = jnp.concatenate([first.astype(bf16), second.astype(bf16)], axis=1)
        move = (src == dst + within).astype(f32).astype(bf16)
        moved = jnp.dot(pair, move, preferred_element_type=f32).astype(bf16)
        blocks += [moved[t * FA : (t + 1) * FA] for t in range(nt)]
    sections = lax.dot_general(
        jnp.concatenate(blocks, axis=1),
        one[...],
        (((0,), (0,)), ((), ())),
        preferred_element_type=f32,
    )
    for k, s in enumerate(chosen):
        last = (two[...].astype(f32) * valid[s].astype(f32)).astype(bf16)
        for t in range(nt):
            at = (k * nt + t) * FB
            re, im = sections[at : at + FB, :FA], sections[at : at + FB, FA:]
            cosine, sine = tcos[...], tsin[...]
            tr = (re * cosine + im * sine).astype(bf16)
            ti = (im * cosine - re * sine).astype(bf16)
            spec = jnp.dot(last, jnp.concatenate([tr, ti], axis=0), preferred_element_type=f32)
            for j in range(FA // LANES):
                a = spec[:NQ, j * LANES : (j + 1) * LANES]
                b = spec[NQ:, j * LANES : (j + 1) * LANES]
                even = jnp.where(low, a, pltpu.roll(b, LO, 1))
                odd = jnp.where(low, pltpu.roll(a, LO, 1), b)
                for h, piece in ((2 * j, even), (2 * j + 1, odd)):
                    to = ((h * nt + t) * stations + s) * OPITCH
                    obuf[pl.ds(pl.multiple_of(to, 8), NQ), :] = piece


def write_messages(nt, at_row, stations, obuf, mbuf, msgs, out_sem):
    per = NQ // PIECES
    sent = []
    for i in range(PIECES):

        def gather(q, _):
            for h in range(NHI):
                got = obuf[
                    pl.ds(h * nt * stations * OPITCH + q, nt * stations, stride=OPITCH), :
                ]
                mbuf[q * NHI + h] = got.astype(bf16)
            return 0

        lax.fori_loop(i * per, (i + 1) * per, gather, 0, unroll=True)
        span = pl.ds(i * per * NHI, per * NHI)
        sent.append(
            pltpu.make_async_copy(
                mbuf.at[span], msgs.at[span, pl.ds(at_row, nt * stations), :], out_sem.at[i]
            )
        )
        sent[i].start()
    for copy in sent:
        copy.wait()


def early_kernel(nt, *refs):
    stream, given, msgs, handed = refs[0], refs[1:7], refs[7], refs[8]
    xin, xs, obuf, mbuf, in_sem, out_sem, small_sem = refs[9:16]
    held = refs[16:]
    stations = stream.shape[0]
    chunk = FA * LANES
    pitch = xs.shape[0] // stations
    copies = [
        pltpu.make_async_copy(
            stream.at[:, pl.ds(i * chunk, chunk)],
            xin.at[:, pl.ds(i * chunk, chunk)],
            in_sem.at[i],
        )
        for i in range(nt + 1)
    ]
    small = [
        pltpu.make_async_copy(source, target, small_sem.at[i])
        for i, (source, target) in enumerate(zip(given, held))
    ]
    for copy in copies + small:
        copy.start()
    for i, copy in enumerate(copies):
        copy.wait()
        spread(xin, i * FA, xs, i * FA, pitch)
    spread(xin, nt * FA, handed, 0, handed.shape[0] // stations)
    xs[pl.ds((nt + 1) * FA, stations, stride=pitch), :] = jnp.zeros((stations, LANES), f32)
    for copy in small:
        copy.wait()

    def group(g, _):
        transform(
            [2 * g, 2 * g + 1], nt, stations, held[0], held[1], held[2:], xs, obuf
        )
        return 0

    lax.fori_loop(0, stations // 2, group, 0, unroll=2)
    write_messages(nt, 0, stations, obuf, mbuf, msgs, out_sem)


def late_kernel(at_row, *refs):
    given, tables, trail = refs[:2], refs[2:6], refs[6]
    xs, msgs, obuf, mbuf, out_sem, small_sem = refs[9:15]
    held = refs[15:]
    stations = trail.shape[0]
    pitch = xs.shape[0] // stations
    small = [
        pltpu.make_async_copy(source, target, small_sem.at[i])
        for i, (source, target) in enumerate(zip(given, held))
    ]
    for copy in small:
        copy.start()
    spread(trail, 0, xs, FA, pitch)
    xs[pl.ds(FA + ROWS, stations, stride=pitch), :] = jnp.zeros((stations, LANES), f32)
    for copy in small:
        copy.wait()
    transform(range(stations), 1, stations, held[0], held[1], tables, xs, obuf)
    write_messages(1, at_row, stations, obuf, mbuf, msgs, out_sem)


def odd_pitch(rows):
    return (rows // 16 + 1) * 16 + 8


def scalars(delays, valid):
    return [pltpu.SMEM(delays.shape, delays.dtype), pltpu.SMEM(valid.shape, valid.dtype)]


def early_messages(stream, delays, valid, tables):
    stations = stream.shape[0]
    far = pl.BlockSpec(memory_space=pltpu.HBM)
    here = stream.shape[1] // (FA * LANES)
    nt = here - 1
    return pl.pallas_call(
        lambda *refs: early_kernel(nt, *refs),
        out_shape=(
            jax.ShapeDtypeStruct((NQ * NHI, here * stations, LANES), bf16),
            pltpu.VMEM((stations * odd_pitch(FA + ROWS), LANES), f32),
        ),
        in_specs=[far] * 7,
        out_specs=(pl.BlockSpec(memory_space=pl.ANY), pl.BlockSpec(memory_space=pltpu.VMEM)),
        scratch_shapes=[
            pltpu.VMEM(stream.shape, bf16),
            pltpu.VMEM((stations * odd_pitch(here * FA), LANES), f32),
            pltpu.VMEM((NHI * nt * stations * OPITCH, LANES), f32),
            pltpu.VMEM((NQ * NHI, nt * stations, LANES), bf16),
            pltpu.SemaphoreType.DMA((here,)),
            pltpu.SemaphoreType.DMA((PIECES,)),
            pltpu.SemaphoreType.DMA((2 + len(tables),)),
        ]
        + scalars(delays, valid)
        + [pltpu.VMEM(table.shape, table.dtype) for table in tables],
        compiler_params=pltpu.CompilerParams(vmem_limit_bytes=28 << 20),
        name="channelize",
    )(*[off_chip(value) for value in (stream, delays, valid, *tables)])


def late_messages(delays, valid, tables, trail, msgs, handed):
    stations = trail.shape[0]
    vmem = pl.BlockSpec(memory_space=pltpu.VMEM)
    hbm = pl.BlockSpec(memory_space=pl.ANY)
    at_row = msgs.shape[1] - stations
    args = [on_chip(value) for value in (delays, valid, *tables, trail, handed)]
    return pl.pallas_call(
        lambda *refs: late_kernel(at_row, *refs),
        out_shape=(
            pltpu.VMEM(handed.shape, f32),
            jax.ShapeDtypeStruct(msgs.shape, bf16),
        ),
        in_specs=[vmem] * 8 + [hbm],
        out_specs=(vmem, hbm),
        scratch_shapes=[
            pltpu.VMEM((NHI * stations * OPITCH, LANES), f32),
            pltpu.VMEM((NQ * NHI, stations, LANES), bf16),
            pltpu.SemaphoreType.DMA((PIECES,)),
            pltpu.SemaphoreType.DMA((2,)),
        ]
        + scalars(delays, valid),
        input_output_aliases={7: 0, 8: 1},
        compiler_params=pltpu.CompilerParams(vmem_limit_bytes=20 << 20),
        name="channelize_late",
    )(*args, msgs)


def tone_kernel(tones, msgs, picks, sums):
    stations, count = tones.shape
    places, rows, _ = msgs.shape

    def add_times(p, _):
        tile = msgs[p].astype(f32)
        total = tile[:stations]
        for t in range(1, rows // stations):
            total = total + tile[t * stations : (t + 1) * stations]
        sums[pl.ds(pl.multiple_of(p * stations, stations), stations), :] = total
        return 0

    lax.fori_loop(0, places, add_times, 0, unroll=8)
    sub = lax.broadcasted_iota(jnp.int32, (stations, LANES), 0)
    slot = lax.broadcasted_iota(jnp.int32, (stations, LANES), 1) % NTONE

    def one_tone(k, acc):
        here = jnp.where(slot == k, sub, -1)
        for s in range(stations):
            chan = tones[s, k]
            place = lax.shift_right_logical(chan, LO.bit_length() - 1)
            within = lax.bitwise_and(chan, LO - 1)
            total = sums[pl.ds(pl.multiple_of(place * stations, stations), stations), :]
            turned = pltpu.roll(total, lax.bitwise_and(k - within, LANES - 1), 1)
            acc = jnp.where(here == s, turned, acc)
        return acc

    picks[...] = lax.fori_loop(0, count, one_tone, jnp.zeros((stations, LANES), f32), unroll=4)


def tone_sums(msgs, tone_chan):
    return pl.pallas_call(
        tone_kernel,
        out_shape=jax.ShapeDtypeStruct((tone_chan.shape[0], 2 * NTONE), f32),
        in_specs=[
            pl.BlockSpec(memory_space=pltpu.SMEM),
            pl.BlockSpec(memory_space=pltpu.VMEM),
        ],
        out_specs=pl.BlockSpec(memory_space=pltpu.VMEM),
        scratch_shapes=[pltpu.VMEM((msgs.shape[0] * tone_chan.shape[0], LANES), f32)],
        compiler_params=pltpu.CompilerParams(vmem_limit_bytes=8 << 20),
        name="tones",
    )(tone_chan, msgs)


PITCH = 136


def x_kernel(norm_scale, per_source, recv, vis, rs, ts, gs, block, out_sem):
    sources, rows, _ = recv.shape
    local = per_source
    groups = S // local
    times = sources // groups * rows // local

    per_group = sources // groups
    for g in range(groups):
        for i in range(g * per_group, (g + 1) * per_group):
            rs[pl.ds(i * rows, rows), :] = recv[i].astype(f32)
        for s in range(local):
            got = rs[pl.ds(g * times * local + s, times, stride=local), :]
            at = (g * local + s) * PITCH
            ts[pl.ds(at, LANES), :] = got.astype(bf16).T.astype(f32)

    lane = lax.broadcasted_iota(jnp.int32, (8, LANES), 1)

    sent = []

    def eight(o, _):
        base = o * 8
        for c in range(8):
            re = ts[pl.ds(base + c, S, stride=PITCH), :]
            im = ts[pl.ds(base + c + LO, S, stride=PITCH), :]
            plus, quad, minus = re.astype(bf16), im.astype(bf16), (-re).astype(bf16)
            straight = jnp.concatenate([plus, quad], axis=1)
            turned = jnp.concatenate([quad, minus], axis=1)
            left = jnp.concatenate([straight, turned], axis=0)
            right = straight
            gram = lax.dot_general(
                left, right, (((1,), (1,)), ((), ())), preferred_element_type=f32
            )
            gs[pl.ds(c * PITCH, 2 * S), :S] = gram * norm_scale
        top = base
        for j in range(S):
            even = gs[pl.ds(2 * j, 8, stride=PITCH), :]
            odd = gs[pl.ds(2 * j + 1, 8, stride=PITCH), :]
            block[pl.ds(top, 8), pl.ds(j * LANES, LANES)] = jnp.where(lane < S, even, pltpu.roll(odd, S, 1))
        return 0

    for o in range(LO // 8):
        eight(o, 0)
        sent.append(
            pltpu.make_async_copy(
                block.at[pl.ds(o * 8, 8), :], vis.at[pl.ds(o * 8, 8), :], out_sem.at[o]
            )
        )
        sent[o].start()
    for copy in sent:
        copy.wait()


def correlated(recv, per_source, norm_scale):
    vmem = pl.BlockSpec(memory_space=pltpu.VMEM)
    return pl.pallas_call(
        lambda *refs: x_kernel(norm_scale, per_source, *refs),
        out_shape=jax.ShapeDtypeStruct((LO, 2 * S * S), f32),
        in_specs=[vmem],
        out_specs=pl.BlockSpec(memory_space=pl.ANY),
        scratch_shapes=[
            pltpu.VMEM((recv.shape[0] * recv.shape[1], LANES), f32),
            pltpu.VMEM((S * PITCH, LANES), f32),
            pltpu.VMEM((8 * PITCH, LANES), f32),
            pltpu.VMEM((LO, 2 * S * S), f32),
            pltpu.SemaphoreType.DMA((LO // 8,)),
        ],
        compiler_params=pltpu.CompilerParams(vmem_limit_bytes=24 << 20),
        name="correlate",
    )(on_chip(recv))


def passed_along(block, axis, distance):
    devices = range(lax.axis_size(axis))
    route = [(i - distance, i) for i in devices if i - distance in devices]
    return lax.ppermute(block, axis, route)


def routed(value, axis, dest):
    return lax.ppermute(value, axis, [(i, dest(i)) for i in range(lax.axis_size(axis))])


def gathered_sum(picks):
    value = picks + routed(picks, "cores", lambda i: i ^ 1)
    value = value + routed(value, "tm", lambda i: i ^ 1)
    size = lax.axis_size("tm")
    half = size // 4
    steps = [
        routed(value, "tm", lambda i, d=d: (i + 2 * (d + half * (i % 2))) % size)
        for d in range(half)
    ]
    value = sum(steps)
    return value + routed(value, "tm", lambda i: i ^ 1)


def shards(samples, delays, valid, tone_chan):
    stations, stretch = samples.shape
    whole = ("stn", "tm", "cores")
    here = stretch // (FA * FB)
    trailing = passed_along(samples[:, :MAXD], ("tm", "cores"), -1)
    tables = [jnp.asarray(table) for table in make_tables()]
    early = early_messages(samples, delays, valid, tables)
    _, msgs = late_messages(delays, valid, tables, trailing, *early)
    spectra_all = here * lax.axis_size("tm") * lax.axis_size("cores")
    norm_scale = 1.0 / math.sqrt(spectra_all)
    recv = lax.all_to_all(msgs, whole, split_axis=0, concat_axis=0, tiled=True)
    phase_cal = gathered_sum(tone_sums(msgs, tone_chan)) * norm_scale
    return (correlated(recv, stations, norm_scale), phase_cal)


def solution(mesh):
    return jax.shard_map(
        shards,
        mesh=mesh,
        in_specs=(P("stn", ("tm", "cores")), P("stn"), P("stn"), P("stn", None)),
        out_specs=(P(("stn", "tm", "cores"), None), P("stn", None)),
        check_vma=False,
    )
```

```python
import math

import jax
import jax.numpy as jnp
import ml_dtypes
import numpy as np
from jax import lax
from jax.experimental import pallas as pl
from jax.experimental.pallas import tpu as pltpu
from jax.sharding import PartitionSpec as P

S = 64
NCH = 16384
FA = 256
FB = 128
NTONE = 64
MAXD = 32768
NQ = FB // 2
NHI = 4
LO = FA // NHI
LANES = 128

f32 = jnp.float32
bf16 = jnp.bfloat16


def make_tables():
    k1 = np.arange(FA)
    angles = 2.0 * np.pi / FA * (k1[:, None] * k1[None, :] % FA)
    section_one = np.concatenate([np.cos(angles), -np.sin(angles)], axis=1).astype(
        ml_dtypes.bfloat16
    )
    n2 = np.arange(FB)
    length = FA * FB
    twists = 2.0 * np.pi / length * (n2[:, None] * k1[None, :] % length)
    scale = 1.0 / math.sqrt(length)
    twist_cos = (np.cos(twists) * scale).astype(np.float32)
    twist_sin = (np.sin(twists) * scale).astype(np.float32)
    q = np.arange(NQ)
    thetas = 2.0 * np.pi / FB * (q[:, None] * n2[None, :] % FB)
    cosine, sine = np.cos(thetas), np.sin(thetas)
    section_two = np.block([[cosine, sine], [-sine, cosine]]).astype(ml_dtypes.bfloat16)
    return (section_one, twist_cos, twist_sin, section_two)


OPITCH = NQ + 8
PIECES = 4
ROWS = MAXD // LANES


def on_chip(value):
    return pltpu.with_memory_space_constraint(value, pltpu.VMEM)


def off_chip(value):
    return pltpu.with_memory_space_constraint(value, pltpu.HBM)


def spread(source, base, xs, first, stride):
    def one_row(j, _):
        at = pl.multiple_of((base + j) * LANES, LANES)
        xs[pl.ds(first + j, source.shape[0], stride=stride), :] = source[
            :, pl.ds(at, LANES)
        ].astype(f32)
        return 0

    lax.fori_loop(0, FA, one_row, 0, unroll=32)


def transform(chosen, nt, stations, delays, valid, tables, xs, obuf):
    one, tcos, tsin, two = tables
    rows = nt * FA
    pitch = xs.shape[0] // stations
    src = lax.broadcasted_iota(jnp.int32, (2 * LANES, LANES), 0)
    dst = lax.broadcasted_iota(jnp.int32, (2 * LANES, LANES), 1)
    low = lax.broadcasted_iota(jnp.int32, (NQ, LANES), 1) < LO
    blocks = []
    for s in chosen:
        shift = delays[s]
        lead = shift // LANES
        within = jnp.where(valid[s] == 0, 2 * LANES, shift - lead * LANES)
        first = xs[pl.ds(s * pitch + lead, rows), :]
        second = xs[pl.ds(s * pitch + lead + 1, rows), :]
        pair = jnp.concatenate([first.astype(bf16), second.astype(bf16)], axis=1)
        move = (src == dst + within).astype(f32).astype(bf16)
        moved = jnp.dot(pair, move, preferred_element_type=f32).astype(bf16)
        blocks += [moved[t * FA : (t + 1) * FA] for t in range(nt)]
    sections = lax.dot_general(
        jnp.concatenate(blocks, axis=1),
        one[...],
        (((0,), (0,)), ((), ())),
        preferred_element_type=f32,
    )
    for k, s in enumerate(chosen):
        for t in range(nt):
            at = (k * nt + t) * FB
            re, im = sections[at : at + FB, :FA], sections[at : at + FB, FA:]
            cosine, sine = tcos[...], tsin[...]
            tr = (re * cosine + im * sine).astype(bf16)
            ti = (im * cosine - re * sine).astype(bf16)
            spec = jnp.dot(
                two[...], jnp.concatenate([tr, ti], axis=0), preferred_element_type=f32
            )
            for j in range(FA // LANES):
                a = spec[:NQ, j * LANES : (j + 1) * LANES]
                b = spec[NQ:, j * LANES : (j + 1) * LANES]
                even = jnp.where(low, a, pltpu.roll(b, LO, 1))
                odd = jnp.where(low, pltpu.roll(a, LO, 1), b)
                for h, piece in ((2 * j, even), (2 * j + 1, odd)):
                    to = ((h * nt + t) * stations + s) * OPITCH
                    obuf[pl.ds(pl.multiple_of(to, 8), NQ), :] = piece


def write_messages(nt, at_row, stations, obuf, mbuf, msgs, out_sem):
    per = NQ // PIECES
    sent = []
    for i in range(PIECES):

        def gather(q, _):
            for h in range(NHI):
                got = obuf[
                    pl.ds(h * nt * stations * OPITCH + q, nt * stations, stride=OPITCH), :
                ]
                mbuf[q * NHI + h] = got.astype(bf16)
            return 0

        lax.fori_loop(i * per, (i + 1) * per, gather, 0, unroll=True)
        span = pl.ds(i * per * NHI, per * NHI)
        sent.append(
            pltpu.make_async_copy(
                mbuf.at[span], msgs.at[span, pl.ds(at_row, nt * stations), :], out_sem.at[i]
            )
        )
        sent[i].start()
    for copy in sent:
        copy.wait()


def early_kernel(nt, *refs):
    stream, given, msgs, handed = refs[0], refs[1:7], refs[7], refs[8]
    xin, xs, obuf, mbuf, in_sem, out_sem, small_sem = refs[9:16]
    held = refs[16:]
    stations = stream.shape[0]
    chunk = FA * LANES
    pitch = xs.shape[0] // stations
    copies = [
        pltpu.make_async_copy(
            stream.at[:, pl.ds(i * chunk, chunk)],
            xin.at[:, pl.ds(i * chunk, chunk)],
            in_sem.at[i],
        )
        for i in range(nt + 1)
    ]
    small = [
        pltpu.make_async_copy(source, target, small_sem.at[i])
        for i, (source, target) in enumerate(zip(given, held))
    ]
    for copy in copies + small:
        copy.start()
    for i, copy in enumerate(copies):
        copy.wait()
        spread(xin, i * FA, xs, i * FA, pitch)
    spread(xin, nt * FA, handed, 0, handed.shape[0] // stations)
    xs[pl.ds((nt + 1) * FA, stations, stride=pitch), :] = jnp.zeros((stations, LANES), f32)
    for copy in small:
        copy.wait()

    def group(g, _):
        transform(
            [2 * g, 2 * g + 1], nt, stations, held[0], held[1], held[2:], xs, obuf
        )
        return 0

    lax.fori_loop(0, stations // 2, group, 0, unroll=2)
    write_messages(nt, 0, stations, obuf, mbuf, msgs, out_sem)


def late_kernel(at_row, *refs):
    given, tables, trail = refs[:2], refs[2:6], refs[6]
    xs, msgs, obuf, mbuf, out_sem, small_sem = refs[9:15]
    held = refs[15:]
    stations = trail.shape[0]
    pitch = xs.shape[0] // stations
    small = [
        pltpu.make_async_copy(source, target, small_sem.at[i])
        for i, (source, target) in enumerate(zip(given, held))
    ]
    for copy in small:
        copy.start()
    spread(trail, 0, xs, FA, pitch)
    xs[pl.ds(FA + ROWS, stations, stride=pitch), :] = jnp.zeros((stations, LANES), f32)
    for copy in small:
        copy.wait()
    transform(range(stations), 1, stations, held[0], held[1], tables, xs, obuf)
    write_messages(1, at_row, stations, obuf, mbuf, msgs, out_sem)


def odd_pitch(rows):
    return (rows // 16 + 1) * 16 + 8


def scalars(delays, valid):
    return [pltpu.SMEM(delays.shape, delays.dtype), pltpu.SMEM(valid.shape, valid.dtype)]


def early_messages(stream, delays, valid, tables):
    stations = stream.shape[0]
    far = pl.BlockSpec(memory_space=pltpu.HBM)
    here = stream.shape[1] // (FA * LANES)
    nt = here - 1
    return pl.pallas_call(
        lambda *refs: early_kernel(nt, *refs),
        out_shape=(
            jax.ShapeDtypeStruct((NQ * NHI, here * stations, LANES), bf16),
            pltpu.VMEM((stations * odd_pitch(FA + ROWS), LANES), f32),
        ),
        in_specs=[far] * 7,
        out_specs=(pl.BlockSpec(memory_space=pl.ANY), pl.BlockSpec(memory_space=pltpu.VMEM)),
        scratch_shapes=[
            pltpu.VMEM(stream.shape, bf16),
            pltpu.VMEM((stations * odd_pitch(here * FA), LANES), f32),
            pltpu.VMEM((NHI * nt * stations * OPITCH, LANES), f32),
            pltpu.VMEM((NQ * NHI, nt * stations, LANES), bf16),
            pltpu.SemaphoreType.DMA((here,)),
            pltpu.SemaphoreType.DMA((PIECES,)),
            pltpu.SemaphoreType.DMA((2 + len(tables),)),
        ]
        + scalars(delays, valid)
        + [pltpu.VMEM(table.shape, table.dtype) for table in tables],
        compiler_params=pltpu.CompilerParams(vmem_limit_bytes=28 << 20),
        name="channelize",
    )(*[off_chip(value) for value in (stream, delays, valid, *tables)])


def late_messages(delays, valid, tables, trail, msgs, handed):
    stations = trail.shape[0]
    vmem = pl.BlockSpec(memory_space=pltpu.VMEM)
    hbm = pl.BlockSpec(memory_space=pl.ANY)
    at_row = msgs.shape[1] - stations
    args = [on_chip(value) for value in (delays, valid, *tables, trail, handed)]
    return pl.pallas_call(
        lambda *refs: late_kernel(at_row, *refs),
        out_shape=(
            pltpu.VMEM(handed.shape, f32),
            jax.ShapeDtypeStruct(msgs.shape, bf16),
        ),
        in_specs=[vmem] * 8 + [hbm],
        out_specs=(vmem, hbm),
        scratch_shapes=[
            pltpu.VMEM((NHI * stations * OPITCH, LANES), f32),
            pltpu.VMEM((NQ * NHI, stations, LANES), bf16),
            pltpu.SemaphoreType.DMA((PIECES,)),
            pltpu.SemaphoreType.DMA((2,)),
        ]
        + scalars(delays, valid),
        input_output_aliases={7: 0, 8: 1},
        compiler_params=pltpu.CompilerParams(vmem_limit_bytes=20 << 20),
        name="channelize_late",
    )(*args, msgs)


def tone_kernel(tones, msgs, picks, sums):
    stations, count = tones.shape
    places, rows, _ = msgs.shape

    def add_times(p, _):
        tile = msgs[p].astype(f32)
        total = tile[:stations]
        for t in range(1, rows // stations):
            total = total + tile[t * stations : (t + 1) * stations]
        sums[pl.ds(pl.multiple_of(p * stations, stations), stations), :] = total
        return 0

    lax.fori_loop(0, places, add_times, 0, unroll=8)
    sub = lax.broadcasted_iota(jnp.int32, (stations, LANES), 0)
    slot = lax.broadcasted_iota(jnp.int32, (stations, LANES), 1) % NTONE

    def one_tone(k, acc):
        here = jnp.where(slot == k, sub, -1)
        for s in range(stations):
            chan = tones[s, k]
            place = lax.shift_right_logical(chan, LO.bit_length() - 1)
            within = lax.bitwise_and(chan, LO - 1)
            total = sums[pl.ds(pl.multiple_of(place * stations, stations), stations), :]
            turned = pltpu.roll(total, lax.bitwise_and(k - within, LANES - 1), 1)
            acc = jnp.where(here == s, turned, acc)
        return acc

    picks[...] = lax.fori_loop(0, count, one_tone, jnp.zeros((stations, LANES), f32), unroll=4)


def tone_sums(msgs, tone_chan):
    return pl.pallas_call(
        tone_kernel,
        out_shape=jax.ShapeDtypeStruct((tone_chan.shape[0], 2 * NTONE), f32),
        in_specs=[
            pl.BlockSpec(memory_space=pltpu.SMEM),
            pl.BlockSpec(memory_space=pltpu.VMEM),
        ],
        out_specs=pl.BlockSpec(memory_space=pltpu.VMEM),
        scratch_shapes=[pltpu.VMEM((msgs.shape[0] * tone_chan.shape[0], LANES), f32)],
        compiler_params=pltpu.CompilerParams(vmem_limit_bytes=8 << 20),
        name="tones",
    )(tone_chan, msgs)


PITCH = 136


def x_kernel(norm_scale, per_source, recv, vis, rs, ts, gs, block, out_sem):
    sources, rows, _ = recv.shape
    local = per_source
    groups = S // local
    times = sources // groups * rows // local

    per_group = sources // groups
    for g in range(groups):
        for i in range(g * per_group, (g + 1) * per_group):
            rs[pl.ds(i * rows, rows), :] = recv[i].astype(f32)
        for s in range(local):
            got = rs[pl.ds(g * times * local + s, times, stride=local), :]
            at = (g * local + s) * PITCH
            ts[pl.ds(at, LANES), :] = got.astype(bf16).T.astype(f32)

    lane = lax.broadcasted_iota(jnp.int32, (8, LANES), 1)

    sent = []

    def eight(o, _):
        base = o * 8
        for c in range(8):
            re = ts[pl.ds(base + c, S, stride=PITCH), :]
            im = ts[pl.ds(base + c + LO, S, stride=PITCH), :]
            plus, quad, minus = re.astype(bf16), im.astype(bf16), (-re).astype(bf16)
            straight = jnp.concatenate([plus, quad], axis=1)
            turned = jnp.concatenate([quad, minus], axis=1)
            left = jnp.concatenate([straight, turned], axis=0)
            right = straight
            gram = lax.dot_general(
                left, right, (((1,), (1,)), ((), ())), preferred_element_type=f32
            )
            gs[pl.ds(c * PITCH, 2 * S), :S] = gram * norm_scale
        top = base
        for j in range(S):
            even = gs[pl.ds(2 * j, 8, stride=PITCH), :]
            odd = gs[pl.ds(2 * j + 1, 8, stride=PITCH), :]
            block[pl.ds(top, 8), pl.ds(j * LANES, LANES)] = jnp.where(lane < S, even, pltpu.roll(odd, S, 1))
        return 0

    for o in range(LO // 8):
        eight(o, 0)
        sent.append(
            pltpu.make_async_copy(
                block.at[pl.ds(o * 8, 8), :], vis.at[pl.ds(o * 8, 8), :], out_sem.at[o]
            )
        )
        sent[o].start()
    for copy in sent:
        copy.wait()


def correlated(recv, per_source, norm_scale):
    vmem = pl.BlockSpec(memory_space=pltpu.VMEM)
    return pl.pallas_call(
        lambda *refs: x_kernel(norm_scale, per_source, *refs),
        out_shape=jax.ShapeDtypeStruct((LO, 2 * S * S), f32),
        in_specs=[vmem],
        out_specs=pl.BlockSpec(memory_space=pl.ANY),
        scratch_shapes=[
            pltpu.VMEM((recv.shape[0] * recv.shape[1], LANES), f32),
            pltpu.VMEM((S * PITCH, LANES), f32),
            pltpu.VMEM((8 * PITCH, LANES), f32),
            pltpu.VMEM((LO, 2 * S * S), f32),
            pltpu.SemaphoreType.DMA((LO // 8,)),
        ],
        compiler_params=pltpu.CompilerParams(vmem_limit_bytes=24 << 20),
        name="correlate",
    )(on_chip(recv))


def passed_along(block, axis, distance):
    devices = range(lax.axis_size(axis))
    route = [(i - distance, i) for i in devices if i - distance in devices]
    return lax.ppermute(block, axis, route)


def routed(value, axis, dest):
    return lax.ppermute(value, axis, [(i, dest(i)) for i in range(lax.axis_size(axis))])


def gathered_sum(picks):
    value = picks + routed(picks, "cores", lambda i: i ^ 1)
    value = value + routed(value, "tm", lambda i: i ^ 1)
    size = lax.axis_size("tm")
    half = size // 4
    steps = [
        routed(value, "tm", lambda i, d=d: (i + 2 * (d + half * (i % 2))) % size)
        for d in range(half)
    ]
    value = sum(steps)
    return value + routed(value, "tm", lambda i: i ^ 1)


def shards(samples, delays, valid, tone_chan):
    stations, stretch = samples.shape
    whole = ("stn", "tm", "cores")
    here = stretch // (FA * FB)
    trailing = passed_along(samples[:, :MAXD], ("tm", "cores"), -1)
    tables = [jnp.asarray(table) for table in make_tables()]
    early = early_messages(samples, delays, valid, tables)
    _, msgs = late_messages(delays, valid, tables, trailing, *early)
    spectra_all = here * lax.axis_size("tm") * lax.axis_size("cores")
    norm_scale = 1.0 / math.sqrt(spectra_all)
    recv = lax.all_to_all(msgs, whole, split_axis=0, concat_axis=0, tiled=True)
    phase_cal = gathered_sum(tone_sums(msgs, tone_chan)) * norm_scale
    return (correlated(recv, stations, norm_scale), phase_cal)


def solution(mesh):
    return jax.shard_map(
        shards,
        mesh=mesh,
        in_specs=(P("stn", ("tm", "cores")), P("stn"), P("stn"), P("stn", None)),
        out_specs=(P(("stn", "tm", "cores"), None), P("stn", None)),
        check_vma=False,
    )
```

```python
import math

import jax
import jax.numpy as jnp
import ml_dtypes
import numpy as np
from jax import lax
from jax.experimental import pallas as pl
from jax.experimental.pallas import tpu as pltpu
from jax.sharding import PartitionSpec as P

S = 64
NCH = 16384
FA = 256
FB = 128
NTONE = 64
MAXD = 32768
NQ = FB // 2
NHI = 4
LO = FA // NHI
LANES = 128

f32 = jnp.float32
bf16 = jnp.bfloat16


def make_tables():
    k1 = np.arange(FA)
    angles = 2.0 * np.pi / FA * (k1[:, None] * k1[None, :] % FA)
    section_one = np.concatenate([np.cos(angles), -np.sin(angles)], axis=1).astype(
        ml_dtypes.bfloat16
    )
    n2 = np.arange(FB)
    length = FA * FB
    twists = 2.0 * np.pi / length * (n2[:, None] * k1[None, :] % length)
    scale = 1.0 / math.sqrt(length)
    twist_cos = (np.cos(twists) * scale).astype(np.float32)
    twist_sin = (np.sin(twists) * scale).astype(np.float32)
    q = np.arange(NQ)
    thetas = 2.0 * np.pi / FB * (q[:, None] * n2[None, :] % FB)
    cosine, sine = np.cos(thetas), np.sin(thetas)
    section_two = np.block([[cosine, sine], [-sine, cosine]]).astype(ml_dtypes.bfloat16)
    return (section_one, twist_cos, twist_sin, section_two)


OPITCH = NQ + 8
PIECES = 4
ROWS = MAXD // LANES


def on_chip(value):
    return pltpu.with_memory_space_constraint(value, pltpu.VMEM)


def off_chip(value):
    return pltpu.with_memory_space_constraint(value, pltpu.HBM)


def spread(source, base, xs, first, stride):
    def one_row(j, _):
        at = pl.multiple_of((base + j) * LANES, LANES)
        xs[pl.ds(first + j, source.shape[0], stride=stride), :] = source[
            :, pl.ds(at, LANES)
        ].astype(f32)
        return 0

    lax.fori_loop(0, FA, one_row, 0, unroll=32)


def transform(chosen, nt, stations, delays, valid, tables, xs, obuf):
    one, tcos, tsin, two = tables
    rows = nt * FA
    pitch = xs.shape[0] // stations
    src = lax.broadcasted_iota(jnp.int32, (2 * LANES, LANES), 0)
    dst = lax.broadcasted_iota(jnp.int32, (2 * LANES, LANES), 1)
    low = lax.broadcasted_iota(jnp.int32, (NQ, LANES), 1) < LO
    blocks = []
    for s in chosen:
        shift = delays[s]
        lead = shift // LANES
        within = jnp.where(valid[s] == 0, 2 * LANES, shift - lead * LANES)
        first = xs[pl.ds(s * pitch + lead, rows), :]
        second = xs[pl.ds(s * pitch + lead + 1, rows), :]
        pair = jnp.concatenate([first.astype(bf16), second.astype(bf16)], axis=1)
        move = (src == dst + within).astype(f32).astype(bf16)
        moved = jnp.dot(pair, move, preferred_element_type=f32).astype(bf16)
        blocks += [moved[t * FA : (t + 1) * FA] for t in range(nt)]
    sections = lax.dot_general(
        jnp.concatenate(blocks, axis=1),
        one[...],
        (((0,), (0,)), ((), ())),
        preferred_element_type=f32,
    )
    for k, s in enumerate(chosen):
        for t in range(nt):
            at = (k * nt + t) * FB
            re, im = sections[at : at + FB, :FA], sections[at : at + FB, FA:]
            cosine, sine = tcos[...], tsin[...]
            tr = (re * cosine + im * sine).astype(bf16)
            ti = (im * cosine - re * sine).astype(bf16)
            spec = jnp.dot(
                two[...], jnp.concatenate([tr, ti], axis=0), preferred_element_type=f32
            )
            for j in range(FA // LANES):
                a = spec[:NQ, j * LANES : (j + 1) * LANES]
                b = spec[NQ:, j * LANES : (j + 1) * LANES]
                even = jnp.where(low, a, pltpu.roll(b, LO, 1))
                odd = jnp.where(low, pltpu.roll(a, LO, 1), b)
                for h, piece in ((2 * j, even), (2 * j + 1, odd)):
                    to = ((h * nt + t) * stations + s) * OPITCH
                    obuf[pl.ds(pl.multiple_of(to, 8), NQ), :] = piece


def write_messages(nt, at_row, stations, obuf, mbuf, msgs, out_sem):
    per = NQ // PIECES
    sent = []
    for i in range(PIECES):

        def gather(q, _):
            for h in range(NHI):
                got = obuf[
                    pl.ds(h * nt * stations * OPITCH + q, nt * stations, stride=OPITCH), :
                ]
                mbuf[q * NHI + h] = got.astype(bf16)
            return 0

        lax.fori_loop(i * per, (i + 1) * per, gather, 0, unroll=True)
        span = pl.ds(i * per * NHI, per * NHI)
        sent.append(
            pltpu.make_async_copy(
                mbuf.at[span], msgs.at[span, pl.ds(at_row, nt * stations), :], out_sem.at[i]
            )
        )
        sent[i].start()
    for copy in sent:
        copy.wait()


def early_kernel(nt, *refs):
    stream, given, msgs, handed = refs[0], refs[1:7], refs[7], refs[8]
    xin, xs, obuf, mbuf, in_sem, out_sem, small_sem = refs[9:16]
    held = refs[16:]
    stations = stream.shape[0]
    chunk = FA * LANES
    pitch = xs.shape[0] // stations
    copies = [
        pltpu.make_async_copy(
            stream.at[:, pl.ds(i * chunk, chunk)],
            xin.at[:, pl.ds(i * chunk, chunk)],
            in_sem.at[i],
        )
        for i in range(nt + 1)
    ]
    small = [
        pltpu.make_async_copy(source, target, small_sem.at[i])
        for i, (source, target) in enumerate(zip(given, held))
    ]
    for copy in copies + small:
        copy.start()
    for i, copy in enumerate(copies):
        copy.wait()
        spread(xin, i * FA, xs, i * FA, pitch)
    spread(xin, nt * FA, handed, 0, handed.shape[0] // stations)
    xs[pl.ds((nt + 1) * FA, stations, stride=pitch), :] = jnp.zeros((stations, LANES), f32)
    for copy in small:
        copy.wait()

    def group(g, _):
        transform(
            [2 * g, 2 * g + 1], nt, stations, held[0], held[1], held[2:], xs, obuf
        )
        return 0

    lax.fori_loop(0, stations // 2, group, 0, unroll=2)
    write_messages(nt, 0, stations, obuf, mbuf, msgs, out_sem)


def late_kernel(at_row, *refs):
    given, tables, trail = refs[:2], refs[2:6], refs[6]
    xs, msgs, obuf, mbuf, out_sem, small_sem = refs[9:15]
    held = refs[15:]
    stations = trail.shape[0]
    pitch = xs.shape[0] // stations
    small = [
        pltpu.make_async_copy(source, target, small_sem.at[i])
        for i, (source, target) in enumerate(zip(given, held))
    ]
    for copy in small:
        copy.start()
    spread(trail, 0, xs, FA, pitch)
    xs[pl.ds(FA + ROWS, stations, stride=pitch), :] = jnp.zeros((stations, LANES), f32)
    for copy in small:
        copy.wait()
    transform(range(stations), 1, stations, held[0], held[1], tables, xs, obuf)
    write_messages(1, at_row, stations, obuf, mbuf, msgs, out_sem)


def odd_pitch(rows):
    return (rows // 16 + 1) * 16 + 8


def scalars(delays, valid):
    return [pltpu.SMEM(delays.shape, delays.dtype), pltpu.SMEM(valid.shape, valid.dtype)]


def early_messages(stream, delays, valid, tables):
    stations = stream.shape[0]
    far = pl.BlockSpec(memory_space=pltpu.HBM)
    here = stream.shape[1] // (FA * LANES)
    nt = here - 1
    return pl.pallas_call(
        lambda *refs: early_kernel(nt, *refs),
        out_shape=(
            jax.ShapeDtypeStruct((NQ * NHI, here * stations, LANES), bf16),
            pltpu.VMEM((stations * odd_pitch(FA + ROWS), LANES), f32),
        ),
        in_specs=[far] * 7,
        out_specs=(pl.BlockSpec(memory_space=pl.ANY), pl.BlockSpec(memory_space=pltpu.VMEM)),
        scratch_shapes=[
            pltpu.VMEM(stream.shape, bf16),
            pltpu.VMEM((stations * odd_pitch(here * FA), LANES), f32),
            pltpu.VMEM((NHI * nt * stations * OPITCH, LANES), f32),
            pltpu.VMEM((NQ * NHI, nt * stations, LANES), bf16),
            pltpu.SemaphoreType.DMA((here,)),
            pltpu.SemaphoreType.DMA((PIECES,)),
            pltpu.SemaphoreType.DMA((2 + len(tables),)),
        ]
        + scalars(delays, valid)
        + [pltpu.VMEM(table.shape, table.dtype) for table in tables],
        compiler_params=pltpu.CompilerParams(vmem_limit_bytes=28 << 20),
        name="channelize",
    )(*[off_chip(value) for value in (stream, delays, valid, *tables)])


def late_messages(delays, valid, tables, trail, msgs, handed):
    stations = trail.shape[0]
    vmem = pl.BlockSpec(memory_space=pltpu.VMEM)
    hbm = pl.BlockSpec(memory_space=pl.ANY)
    at_row = msgs.shape[1] - stations
    args = [on_chip(value) for value in (delays, valid, *tables, trail, handed)]
    return pl.pallas_call(
        lambda *refs: late_kernel(at_row, *refs),
        out_shape=(
            pltpu.VMEM(handed.shape, f32),
            jax.ShapeDtypeStruct(msgs.shape, bf16),
        ),
        in_specs=[vmem] * 8 + [hbm],
        out_specs=(vmem, hbm),
        scratch_shapes=[
            pltpu.VMEM((NHI * stations * OPITCH, LANES), f32),
            pltpu.VMEM((NQ * NHI, stations, LANES), bf16),
            pltpu.SemaphoreType.DMA((PIECES,)),
            pltpu.SemaphoreType.DMA((2,)),
        ]
        + scalars(delays, valid),
        input_output_aliases={7: 0, 8: 1},
        compiler_params=pltpu.CompilerParams(vmem_limit_bytes=20 << 20),
        name="channelize_late",
    )(*args, msgs)


def tone_kernel(tones, msgs, picks, sums):
    stations, count = tones.shape
    places, rows, _ = msgs.shape

    def add_times(p, _):
        tile = msgs[p].astype(f32)
        total = tile[:stations]
        for t in range(1, rows // stations):
            total = total + tile[t * stations : (t + 1) * stations]
        sums[pl.ds(pl.multiple_of(p * stations, stations), stations), :] = total
        return 0

    lax.fori_loop(0, places, add_times, 0, unroll=8)
    sub = lax.broadcasted_iota(jnp.int32, (stations, LANES), 0)
    slot = lax.broadcasted_iota(jnp.int32, (stations, LANES), 1) % NTONE

    def one_tone(k, acc):
        here = jnp.where(slot == k, sub, -1)
        for s in range(stations):
            chan = tones[s, k]
            place = lax.shift_right_logical(chan, LO.bit_length() - 1)
            within = lax.bitwise_and(chan, LO - 1)
            total = sums[pl.ds(pl.multiple_of(place * stations, stations), stations), :]
            turned = pltpu.roll(total, lax.bitwise_and(k - within, LANES - 1), 1)
            acc = jnp.where(here == s, turned, acc)
        return acc

    picks[...] = lax.fori_loop(0, count, one_tone, jnp.zeros((stations, LANES), f32), unroll=4)


def tone_sums(msgs, tone_chan):
    return pl.pallas_call(
        tone_kernel,
        out_shape=jax.ShapeDtypeStruct((tone_chan.shape[0], 2 * NTONE), f32),
        in_specs=[
            pl.BlockSpec(memory_space=pltpu.SMEM),
            pl.BlockSpec(memory_space=pltpu.VMEM),
        ],
        out_specs=pl.BlockSpec(memory_space=pltpu.VMEM),
        scratch_shapes=[pltpu.VMEM((msgs.shape[0] * tone_chan.shape[0], LANES), f32)],
        compiler_params=pltpu.CompilerParams(vmem_limit_bytes=8 << 20),
        name="tones",
    )(tone_chan, msgs)


PITCH = 136


def x_kernel(norm_scale, per_source, recv, vis, rs, ts, gs, block, out_sem):
    sources, rows, _ = recv.shape
    local = per_source
    groups = S // local
    times = sources // groups * rows // local

    per_group = sources // groups
    for g in range(groups):
        for i in range(g * per_group, (g + 1) * per_group):
            rs[pl.ds(i * rows, rows), :] = recv[i].astype(f32)
        for s in range(local):
            got = rs[pl.ds(g * times * local + s, times, stride=local), :]
            at = (g * local + s) * PITCH
            ts[pl.ds(at, LANES), :] = got.astype(bf16).T.astype(f32)

    lane = lax.broadcasted_iota(jnp.int32, (8, LANES), 1)

    sent = []

    def eight(o, _):
        base = o * 8
        for c in range(8):
            re = ts[pl.ds(base + c, S, stride=PITCH), :]
            im = ts[pl.ds(base + c + LO, S, stride=PITCH), :]
            plus, quad, minus = re.astype(bf16), im.astype(bf16), (-re).astype(bf16)
            straight = jnp.concatenate([plus, quad], axis=1)
            turned = jnp.concatenate([quad, minus], axis=1)
            left = jnp.concatenate([straight, turned], axis=0)
            right = straight
            gram = lax.dot_general(
                left, right, (((1,), (1,)), ((), ())), preferred_element_type=f32
            )
            gs[pl.ds(c * PITCH, 2 * S), :S] = gram * norm_scale
        top = base
        for j in range(S):
            even = gs[pl.ds(2 * j, 8, stride=PITCH), :]
            odd = gs[pl.ds(2 * j + 1, 8, stride=PITCH), :]
            block[pl.ds(top, 8), pl.ds(j * LANES, LANES)] = jnp.where(lane < S, even, pltpu.roll(odd, S, 1))
        return 0

    for o in range(LO // 8):
        eight(o, 0)
        for part in range(2):
            span = (pl.ds(o * 8, 8), pl.ds(part * S * S, S * S))
            sent.append(
                pltpu.make_async_copy(block.at[span], vis.at[span], out_sem.at[2 * o + part])
            )
            sent[-1].start()
    for copy in sent:
        copy.wait()


def correlated(recv, per_source, norm_scale):
    vmem = pl.BlockSpec(memory_space=pltpu.VMEM)
    return pl.pallas_call(
        lambda *refs: x_kernel(norm_scale, per_source, *refs),
        out_shape=jax.ShapeDtypeStruct((LO, 2 * S * S), f32),
        in_specs=[vmem],
        out_specs=pl.BlockSpec(memory_space=pl.ANY),
        scratch_shapes=[
            pltpu.VMEM((recv.shape[0] * recv.shape[1], LANES), f32),
            pltpu.VMEM((S * PITCH, LANES), f32),
            pltpu.VMEM((8 * PITCH, LANES), f32),
            pltpu.VMEM((LO, 2 * S * S), f32),
            pltpu.SemaphoreType.DMA((LO // 4,)),
        ],
        compiler_params=pltpu.CompilerParams(vmem_limit_bytes=24 << 20),
        name="correlate",
    )(on_chip(recv))


def passed_along(block, axis, distance):
    devices = range(lax.axis_size(axis))
    route = [(i - distance, i) for i in devices if i - distance in devices]
    return lax.ppermute(block, axis, route)


def routed(value, axis, dest):
    return lax.ppermute(value, axis, [(i, dest(i)) for i in range(lax.axis_size(axis))])


def gathered_sum(picks):
    value = picks + routed(picks, "cores", lambda i: i ^ 1)
    value = value + routed(value, "tm", lambda i: i ^ 1)
    size = lax.axis_size("tm")
    half = size // 4
    steps = [
        routed(value, "tm", lambda i, d=d: (i + 2 * (d + half * (i % 2))) % size)
        for d in range(half)
    ]
    value = sum(steps)
    return value + routed(value, "tm", lambda i: i ^ 1)


def shards(samples, delays, valid, tone_chan):
    stations, stretch = samples.shape
    whole = ("stn", "tm", "cores")
    here = stretch // (FA * FB)
    trailing = passed_along(samples[:, :MAXD], ("tm", "cores"), -1)
    tables = [jnp.asarray(table) for table in make_tables()]
    early = early_messages(samples, delays, valid, tables)
    _, msgs = late_messages(delays, valid, tables, trailing, *early)
    spectra_all = here * lax.axis_size("tm") * lax.axis_size("cores")
    norm_scale = 1.0 / math.sqrt(spectra_all)
    recv = lax.all_to_all(msgs, whole, split_axis=0, concat_axis=0, tiled=True)
    phase_cal = gathered_sum(tone_sums(msgs, tone_chan)) * norm_scale
    return (correlated(recv, stations, norm_scale), phase_cal)


def solution(mesh):
    return jax.shard_map(
        shards,
        mesh=mesh,
        in_specs=(P("stn", ("tm", "cores")), P("stn"), P("stn"), P("stn", None)),
        out_specs=(P(("stn", "tm", "cores"), None), P("stn", None)),
        check_vma=False,
    )
```
